512 devices in a mesh: lon: 128 (over z_hi, x, y, core), lev: 4 (over z_lo).
Axes of the slice: x: 4, y: 8, z: 8 (z_hi: 2, z_lo: 4; z = z_hi * 4 + z_lo), core: 2. Of those that a mesh axis runs over, the one named last changes fastest.
Arguments:
- thickness: float32 [4, 2048, 2048], P('lev', 'lon'), may hold values from 0.5 to 1.5
- wind_field: float32 [2, 4, 2048, 2048], P(None, 'lev', 'lon'), may hold values from -3 to 3
Outputs:
- new_thickness: float32 [4, 2048, 2048], P('lev', 'lon')
- new_winds: float32 [2, 4, 2048, 2048], P(None, 'lev', 'lon')
The draws below stay inside these ranges and needn't reach their ends.
All inputs are finite; a program needn't handle non-finite values.
Results may differ from the reference program's by a relative error of at most 0.0001.
Values sent between devices are 32-bit elements; how exact they have to be, the bound alone decides.
A program may use at most 64 MiB of HBM per device.

```python
import math
import jax
import jax.numpy as jnp
from jax import lax

NLAT = 2048
STEPS = 2
NLON = 2048
LEV = 4
KMAX = 1365


def block_levels(key, shape, shards, smallest, high):
    gain = 1.0
    for dim, shards_of in shards:
        steps = jax.random.uniform(jax.random.fold_in(jax.random.fold_in(key, 6), dim), (shards_of,), jnp.float32, smallest / len(shards), high / len(shards))
        gain = gain * jnp.repeat(jnp.exp(steps), shape[dim] // shards_of).reshape((-1,) + (1,) * (len(shape) - 1 - dim))
    return gain


def gaussian(key, shape, deviation, limit, shards=(), held_as=jnp.bfloat16):
    level = block_levels(key, shape, shards, -0.22, 0.18) if shards else 1.0
    entries = jax.random.normal(key, shape, jnp.float32) * deviation * level
    return jnp.minimum(jnp.maximum(entries, -limit), limit).astype(held_as)


def setup_inputs(seed: int = 0) -> dict:
    key_of = jax.random.split(jax.random.key(seed), 3)
    thickness = jnp.clip(0.5 + 1.0 * jax.random.uniform(key_of[0], (LEV, NLON, NLAT), jnp.float32) ** block_levels(key_of[0], (LEV, NLON, NLAT), ((0, 4), (1, 128)), -0.2, 0.2), 0.5, 1.5)
    wind_field = gaussian(key_of[1], (2, LEV, NLON, NLAT), 0.5, 3.0, ((1, 4), (2, 128)), jnp.float32)
    return dict(thickness=thickness, wind_field=wind_field)


courant = 0.2
mixing = 0.25
coriolis = 0.5
cos_floor = 0.25
lon_weights = ((1, 45.0), (2, -9.0), (3, 1.0))


def lon_derivative(fields, axis_index):
    summed = jnp.zeros_like(fields)
    for offset, weight in lon_weights:
        summed = summed + weight * (jnp.roll(fields, -offset, axis_index) - jnp.roll(fields, offset, axis_index))
    return summed / 60.0


def spectral(fields):
    sign_column = jnp.array([1.0, -1.0, -1.0], dtype=fields.dtype).reshape(3, 1, 1)
    antipode = jnp.roll(fields, NLON // 2, 1)
    circle = jnp.concatenate([fields, sign_column * antipode[:, :, ::-1]], 2)
    length = 2 * NLAT
    spectrum = jnp.fft.rfft(circle, axis=2)
    wavenumbers = jnp.arange(NLAT + 1).astype(fields.dtype)
    retained = (wavenumbers <= KMAX).astype(fields.dtype)
    smooth = jnp.fft.irfft(spectrum * retained, n=length, axis=2)[:, :, :NLAT]
    factor = (2.0 * math.pi / length) * wavenumbers * retained
    meridional_slope = jnp.fft.irfft(spectrum * (1j * factor), n=length, axis=2)[:, :, :NLAT]
    return smooth.astype(fields.dtype), meridional_slope.astype(fields.dtype)


def level_update(fields, vertical, secant, coriolis_term):
    smooth, meridional_slope = spectral(fields)
    zonal_slope = lon_derivative(fields, 1)
    thickness_now = fields[0]
    eastward = fields[1]
    northward = fields[2]
    advect = eastward * secant * zonal_slope + northward * meridional_slope
    height_tendency = -advect[0] - thickness_now * (secant * zonal_slope[1] + meridional_slope[2]) + mixing * vertical
    east_tendency = -advect[1] - secant * zonal_slope[0] + coriolis_term * northward
    north_tendency = -advect[2] - meridional_slope[0] - coriolis_term * eastward
    return smooth + courant * jnp.stack([height_tendency, east_tendency, north_tendency])


def reference(thickness, wind_field):
    latitude = (jnp.arange(NLAT).astype(jnp.float32) + 0.5) * (math.pi / NLAT) - 0.5 * math.pi
    secant = 1.0 / jnp.maximum(jnp.cos(latitude), cos_floor)
    coriolis_term = coriolis * jnp.sin(latitude)
    fields_now = jnp.concatenate([thickness[None], wind_field], 0)
    for step_index in range(STEPS):
        padded = jnp.pad(fields_now[0], ((1, 1), (0, 0), (0, 0)))
        vertical = padded[2:] + padded[:-2] - 2.0 * fields_now[0]
        updated = lax.map(lambda level_pair: level_update(level_pair[0], level_pair[1], secant, coriolis_term), (jnp.swapaxes(fields_now, 0, 1), vertical))
        fields_now = jnp.swapaxes(updated, 0, 1)
    return fields_now[0], fields_now[1:]
```

```python
import functools
import math

import jax
import jax.numpy as jnp
import numpy as np
from jax import lax
from jax.experimental import pallas as pl
from jax.experimental.pallas import tpu as pltpu
from jax.sharding import PartitionSpec as P

STEPS = 2
MESH = pl.DeviceIdType.MESH

courant = 0.2
mixing = 0.25
coriolis = 0.5
cos_floor = 0.25

LANES = 128
ROWS = 8
f32 = jnp.float32
bf16 = jnp.bfloat16


def rotate(z, angle):
    re, im = z
    c, s = math.cos(angle), math.sin(angle)
    if abs(s) < 1e-12:
        return (re, im) if c > 0 else (-re, -im)
    if abs(c) < 1e-12:
        return (-im, re) if s > 0 else (im, -re)
    return re * c - im * s, re * s + im * c


def complex_sum(values, sign):
    count = len(values)
    if count == 1:
        return values
    half = count // 2
    plus = [(a[0] + b[0], a[1] + b[1]) for a, b in zip(values[:half], values[half:])]
    minus = [(a[0] - b[0], a[1] - b[1]) for a, b in zip(values[:half], values[half:])]
    minus = [rotate(z, sign * 2 * math.pi * n / count) for n, z in enumerate(minus)]
    even, odd = complex_sum(plus, sign), complex_sum(minus, sign)
    return [z for pair in zip(even, odd) for z in pair]


def odd_frequencies(values):
    count = len(values)
    if count == 1:
        return {1: (values[0], None)}
    half = count // 2
    joined = [rotate((values[n], -values[n + half]), -math.pi * n / count) for n in range(half)]
    out = {}
    for t, (re, im) in enumerate(complex_sum(joined, -1)):
        k = 4 * t + 1
        if k <= count:
            out[k] = (re, im)
        else:
            out[2 * count - k] = (re, -im)
    return out


def real_transform(values):
    count = len(values)
    if count == 1:
        return {0: (values[0], None)}
    half = count // 2
    even = real_transform([values[n] + values[n + half] for n in range(half)])
    out = {2 * k: z for k, z in even.items()}
    out.update(odd_frequencies([values[n] - values[n + half] for n in range(half)]))
    return out


def padded_transform(values):
    out = {2 * k: z for k, z in real_transform(values).items()}
    out.update(odd_frequencies(values))
    return out


def odd_inverse(terms, count):
    if count == 1:
        return [terms[1][0]]
    half = count // 2
    joined = []
    for t in range(half):
        k = 4 * t + 1
        if k <= count:
            joined.append(terms[k])
        else:
            re, im = terms[2 * count - k]
            joined.append((re, -im))
    turned = [rotate(z, math.pi * n / count) for n, z in enumerate(complex_sum(joined, 1))]
    return [z[0] for z in turned] + [-z[1] for z in turned]


def real_inverse(terms, count):
    if count == 1:
        return [terms[0][0]]
    half = count // 2
    even = real_inverse({k // 2: z for k, z in terms.items() if k % 2 == 0}, half)
    odd = odd_inverse({k: z for k, z in terms.items() if k % 2}, half)
    return [a + b for a, b in zip(even, odd)] + [a - b for a, b in zip(even, odd)]


def padded_inverse(terms, count):
    even = real_inverse({k // 2: z for k, z in terms.items() if k % 2 == 0}, count)
    odd = odd_inverse({k: z for k, z in terms.items() if k % 2}, count)
    return [a + b for a, b in zip(even, odd)]


def split(value):
    high = value.astype(bf16)
    return high, (value - high.astype(f32)).astype(bf16)


def np_split(table):
    table = jnp.asarray(table.astype(np.float32))
    high = table.astype(bf16)
    return high, (table - high.astype(f32)).astype(bf16)


def tables(lat_count, lon_count):
    length = 2 * lat_count
    blocks = lat_count // LANES
    ring = 2 * blocks
    kept = length // 3
    reach = kept // ring + 1
    lane = np.arange(LANES)
    shift = np.where(lane < 2 * reach, lane - reach, 0)
    valid = (lane < 2 * reach).astype(np.float64)
    psi = 2 * np.pi * (lane[:, None] + 0.5) * shift[None, :] / LANES
    cos, sin = np.cos(psi) * valid, np.sin(psi) * valid
    forward = np.block([[cos, sin], [sin, -cos]])
    inverse = np.block([[cos.T, sin.T], [sin.T, -cos.T]])
    small = np.arange(blocks + 1)
    phi = 2 * np.pi * small[:, None] * (lane[None, :] + 0.5) / length
    twist = np.concatenate([np.cos(phi), np.sin(phi)], 1)
    index = small[:, None] + ring * shift[None, :]
    weight = np.where((small == 0) | (small == blocks), 1.0, 2.0)[:, None] / length
    weight = weight * (np.abs(index) <= kept) * valid
    slope = weight * 2 * np.pi * index / length
    factor = np.concatenate([weight, weight, slope, -slope], 1)
    latitude = (np.arange(lat_count) + 0.5) * (np.pi / lat_count) - 0.5 * np.pi
    secant = 1.0 / np.maximum(np.cos(latitude), cos_floor)
    line = np.zeros((8, lat_count))
    line[0] = secant / 60.0
    line[1] = coriolis * np.sin(latitude)
    fields = 3
    own = np.zeros((fields * lon_count, fields * lon_count))
    outer = np.zeros((fields * lon_count, 2 * fields * ROWS))
    for f in range(fields):
        for row in range(lon_count):
            for offset, value in ((1, 45.0), (2, -9.0), (3, 1.0)):
                for sign in (1, -1):
                    at = row + sign * offset
                    if at < 0:
                        outer[f * lon_count + row, f * ROWS + at + ROWS] = sign * value
                    elif at >= lon_count:
                        outer[f * lon_count + row, (fields + f) * ROWS + at - lon_count] = sign * value
                    else:
                        own[f * lon_count + row, f * lon_count + at] = sign * value
    own = np.concatenate([own, own], 1)
    outer = np.concatenate([outer, outer], 1)
    return (
        *np_split(forward),
        *np_split(inverse),
        jnp.asarray(twist.astype(np.float32)),
        jnp.asarray(factor.astype(np.float32)),
        jnp.asarray(line.astype(np.float32)),
        jnp.asarray(own.astype(np.float32)).astype(bf16),
        jnp.asarray(outer.astype(np.float32)).astype(bf16),
    )


def kernel(
    sizes, thick_ref, wind_ref, fwd_hi, fwd_lo, inv_hi, inv_lo, twist_ref, factor_ref, line_ref, own_ref, outer_ref,
    out_h, out_w, state, opposite, halo, levels, spec_in, gain_own, turned, zonal, smooth, slope, load_sem,
    anti_send, anti_recv, halo_send, halo_recv, lev_send, lev_recv,
):
    lon_size, lev_size = sizes
    fields, lon_count, lat_count = state.shape[1:]
    blocks = lat_count // LANES
    groups = lon_count // ROWS
    lon, lev = lax.axis_index("lon"), lax.axis_index("lev")
    right = lax.rem(lon + 1, lon_size)
    left = lax.rem(lon + lon_size - 1, lon_size)
    partner = lax.rem(lon + lon_size // 2, lon_size)
    has_below, has_above = lev > 0, lev < lev_size - 1

    loads = [pltpu.make_async_copy(thick_ref.at[0], state.at[0, 0], load_sem.at[0])]
    loads += [pltpu.make_async_copy(wind_ref.at[f, 0], state.at[0, f + 1], load_sem.at[f + 1]) for f in range(2)]
    for copy in loads:
        copy.start()
    halo[...] = jnp.zeros_like(halo)

    @pl.when(jnp.logical_not(has_below))
    def _():
        for s in range(STEPS):
            levels[s, 0] = jnp.zeros_like(levels[s, 0])

    @pl.when(jnp.logical_not(has_above))
    def _():
        for s in range(STEPS):
            levels[s, 1] = jnp.zeros_like(levels[s, 1])

    barrier = pltpu.get_barrier_semaphore()
    for at in (left, right, partner):
        pl.semaphore_signal(barrier, inc=1, device_id={"lon": at}, device_id_type=MESH)

    @pl.when(has_below)
    def _():
        pl.semaphore_signal(barrier, inc=1, device_id={"lev": lev - 1}, device_id_type=MESH)

    @pl.when(has_above)
    def _():
        pl.semaphore_signal(barrier, inc=1, device_id={"lev": lev + 1}, device_id_type=MESH)

    pl.semaphore_wait(barrier, 3 + has_below.astype(jnp.int32) + has_above.astype(jnp.int32))

    def rows(g):
        return pl.ds(g * ROWS, ROWS)

    def source(s, f, at):
        if s == 0:
            return thick_ref.at[0, at] if f == 0 else wind_ref.at[f - 1, 0, at]
        return state.at[s, f, at]

    def anti_copy(s, g, f):
        return pltpu.make_async_remote_copy(
            src_ref=source(s, f, rows(g)), dst_ref=opposite.at[s, f, rows(g)],
            send_sem=anti_send.at[s, g, f], recv_sem=anti_recv.at[s, g, f],
            device_id={"lon": partner}, device_id_type=MESH,
        )

    def halo_copy(s, side, f):
        start = lon_count - 3 if side == 0 else 0
        landing = ROWS - 3 if side == 0 else 0
        return pltpu.make_async_remote_copy(
            src_ref=source(s, f, pl.ds(start, 3)), dst_ref=halo.at[s, side, f, pl.ds(landing, 3)],
            send_sem=halo_send.at[s, side, f], recv_sem=halo_recv.at[s, side, f],
            device_id={"lon": right if side == 0 else left}, device_id_type=MESH,
        )

    def lev_copy(s, g, side):
        return pltpu.make_async_remote_copy(
            src_ref=source(s, 0, rows(g)), dst_ref=levels.at[s, side, rows(g)],
            send_sem=lev_send.at[s, g, side], recv_sem=lev_recv.at[s, g, side],
            device_id={"lev": lev + 1 if side == 0 else lev - 1}, device_id_type=MESH,
        )

    def send_halo(s, side):
        for f in range(fields):
            halo_copy(s, side, f).start()

    def send_group(s, g):
        for f in range(fields):
            anti_copy(s, g, f).start()

        @pl.when(has_above)
        def _():
            lev_copy(s, g, 0).start()

        @pl.when(has_below)
        def _():
            lev_copy(s, g, 1).start()

    def transform_half(ref, s, g):
        for f in range(fields):
            values = [ref[s, f, g * ROWS : (g + 1) * ROWS, n * LANES : (n + 1) * LANES] for n in range(blocks)]
            for k, (re, im) in padded_transform(values).items():
                at = (k * fields + f) * ROWS
                c, d = twist_ref[k : k + 1, :LANES], twist_ref[k : k + 1, LANES:]
                if k == 0:
                    out = (re, jnp.zeros_like(re))
                elif im is None:
                    out = (re * c, -re * d)
                else:
                    out = (re * c + im * d, im * c - re * d)
                spec_in[at : at + ROWS, :LANES] = out[0]
                spec_in[at : at + ROWS, LANES:] = out[1]
        return product(spec_in[...], fwd_hi, fwd_lo)

    def product(value, high, low):
        top, rest = split(value)
        out = jnp.dot(top, low[...], preferred_element_type=f32)
        out += jnp.dot(rest, high[...], preferred_element_type=f32)
        return out + jnp.dot(top, high[...], preferred_element_type=f32)

    def own_group(s, g):
        gain_own[g] = transform_half(state, s, g)

    def own_zonal(s):
        value = state[s].reshape(fields * lon_count, lat_count)
        zonal[...] = jnp.dot(own_ref[...], jnp.concatenate(split(value), 0), preferred_element_type=f32)

    def outer_zonal(s):
        for side in range(2):
            for f in range(fields):
                halo_copy(s, side, f).wait_recv()
        value = halo[s].reshape(2 * fields * ROWS, lat_count)
        zonal[...] += jnp.dot(outer_ref[...], jnp.concatenate(split(value), 0), preferred_element_type=f32)

    def back(g, which):
        target = smooth if which == 0 else slope
        for f in range(fields):
            terms = {}
            for k in range(blocks + 1):
                at = (k * fields + f) * ROWS
                re, im = turned[which, at : at + ROWS, :LANES], turned[which, at : at + ROWS, LANES:]
                c, d = twist_ref[k : k + 1, :LANES], twist_ref[k : k + 1, LANES:]
                if k == 0:
                    terms[k] = (re, None)
                elif k == blocks:
                    terms[k] = (re * c - im * d, None)
                else:
                    terms[k] = (re * c - im * d, re * d + im * c)
            for n, value in enumerate(padded_inverse(terms, blocks)):
                target[f, :, n * LANES : (n + 1) * LANES] = value

    def group(s, g):
        for f in range(fields):
            anti_copy(s, g, f).wait_recv()
        theirs = transform_half(opposite, s, g)
        mine = gain_own[g]
        first, second = [], []
        for k in range(blocks + 1):
            for f in range(fields):
                at = (k * fields + f) * ROWS
                sign = 1.0 if f == 0 else -1.0
                a = mine[at : at + ROWS, :LANES] + sign * theirs[at : at + ROWS, :LANES]
                b = mine[at : at + ROWS, LANES:] - sign * theirs[at : at + ROWS, LANES:]
                w = factor_ref[k : k + 1]
                turned[0, at : at + ROWS, :LANES] = a * w[:, :LANES]
                turned[0, at : at + ROWS, LANES:] = b * w[:, LANES : 2 * LANES]
                turned[1, at : at + ROWS, :LANES] = b * w[:, 2 * LANES : 3 * LANES]
                turned[1, at : at + ROWS, LANES:] = a * w[:, 3 * LANES :]
        for which in range(2):
            turned[which] = product(turned[which], inv_hi, inv_lo)
        for which in range(2):
            back(g, which)

        @pl.when(has_below)
        def _():
            lev_copy(s, g, 0).wait_recv()

        @pl.when(has_above)
        def _():
            lev_copy(s, g, 1).wait_recv()

        r = slice(g * ROWS, (g + 1) * ROWS)
        for n in range(blocks):
            lanes = slice(n * LANES, (n + 1) * LANES)
            h, u, v = (state[s, f, r, lanes] for f in range(fields))
            secant, turn = line_ref[0:1, lanes], line_ref[1:2, lanes]
            zh, zu, zv = (
                zonal[f * lon_count + g * ROWS : f * lon_count + (g + 1) * ROWS, lanes] * secant for f in range(fields)
            )
            mh, mu, mv = (slope[f, :, lanes] for f in range(fields))
            vertical = levels[s, 0, r, lanes] + levels[s, 1, r, lanes] - 2.0 * h
            th = mixing * vertical - (u * zh + v * mh) - h * (zu + mv)
            tu = turn * v - (u * zu + v * mu) - zh
            tv = -(u * zv + v * mv) - mh - turn * u
            nh, nu, nv = (smooth[f, :, lanes] + courant * t for f, t in enumerate((th, tu, tv)))
            if s < STEPS - 1:
                state[s + 1, 0, r, lanes] = nh
                state[s + 1, 1, r, lanes] = nu
                state[s + 1, 2, r, lanes] = nv
            else:
                out_h[0, r, lanes] = nh
                out_w[0, 0, r, lanes] = nu
                out_w[1, 0, r, lanes] = nv

    send_halo(0, 0)
    send_halo(0, 1)
    for g in range(groups):
        send_group(0, g)
    for copy in loads:
        copy.wait()
    for s in range(STEPS):
        if s == 0:
            own_group(s, 0)
        own_group(s, groups - 1)
        own_zonal(s)
        outer_zonal(s)
        for g in range(groups):
            group(s, g)
            if s < STEPS - 1:
                send_group(s + 1, g)
                if g == 0:
                    send_halo(s + 1, 1)
                    own_group(s + 1, 0)
                else:
                    send_halo(s + 1, 0)
    for s in range(STEPS):
        for g in range(groups):
            for f in range(fields):
                anti_copy(s, g, f).wait_send()

            @pl.when(has_above)
            def _():
                lev_copy(s, g, 0).wait_send()

            @pl.when(has_below)
            def _():
                lev_copy(s, g, 1).wait_send()

        for side in range(2):
            for f in range(fields):
                halo_copy(s, side, f).wait_send()


def body(sizes, thickness, wind_field):
    level_count, lon_count, lat_count = thickness.shape
    fields = 3
    groups = lon_count // ROWS
    blocks = lat_count // LANES
    spectral_rows = (blocks + 1) * fields * ROWS
    consts = tables(lat_count, lon_count)
    vmem = pl.BlockSpec(memory_space=pltpu.VMEM)
    hbm = pl.BlockSpec(memory_space=pl.ANY)
    dma = pltpu.SemaphoreType.DMA
    return pl.pallas_call(
        functools.partial(kernel, sizes),
        out_shape=(
            jax.ShapeDtypeStruct(thickness.shape, f32),
            jax.ShapeDtypeStruct(wind_field.shape, f32),
        ),
        in_specs=[hbm, hbm] + [vmem] * len(consts),
        out_specs=(vmem, vmem),
        scratch_shapes=[
            pltpu.VMEM((STEPS, fields, lon_count, lat_count), f32),
            pltpu.VMEM((STEPS, fields, lon_count, lat_count), f32),
            pltpu.VMEM((STEPS, 2, fields, ROWS, lat_count), f32),
            pltpu.VMEM((STEPS, 2, lon_count, lat_count), f32),
            pltpu.VMEM((spectral_rows, 2 * LANES), f32),
            pltpu.VMEM((groups, spectral_rows, 2 * LANES), f32),
            pltpu.VMEM((2, spectral_rows, 2 * LANES), f32),
            pltpu.VMEM((fields * lon_count, lat_count), f32),
            pltpu.VMEM((fields, ROWS, lat_count), f32),
            pltpu.VMEM((fields, ROWS, lat_count), f32),
            dma((fields,)),
            dma((STEPS, groups, fields)),
            dma((STEPS, groups, fields)),
            dma((STEPS, 2, fields)),
            dma((STEPS, 2, fields)),
            dma((STEPS, groups, 2)),
            dma((STEPS, groups, 2)),
        ],
        name="sphere_steps",
        compiler_params=pltpu.CompilerParams(collective_id=0, has_side_effects=True, vmem_limit_bytes=40 << 20),
    )(thickness, wind_field, *consts)


def solution(mesh):
    sizes = (mesh.shape["lon"], mesh.shape["lev"])
    in_specs = (P("lev", "lon", None), P(None, "lev", "lon", None))
    out_specs = (P("lev", "lon", None), P(None, "lev", "lon", None))
    return jax.shard_map(
        functools.partial(body, sizes), mesh=mesh, in_specs=in_specs, out_specs=out_specs, check_vma=False
    )
```

```python
import functools
import math

import jax
import jax.numpy as jnp
import numpy as np
from jax import lax
from jax.experimental import pallas as pl
from jax.experimental.pallas import tpu as pltpu
from jax.sharding import PartitionSpec as P

STEPS = 2
MESH = pl.DeviceIdType.MESH

courant = 0.2
mixing = 0.25
coriolis = 0.5
cos_floor = 0.25

LANES = 128
ROWS = 8
f32 = jnp.float32
bf16 = jnp.bfloat16


def rotate(z, angle):
    re, im = z
    c, s = math.cos(angle), math.sin(angle)
    if abs(s) < 1e-12:
        return (re, im) if c > 0 else (-re, -im)
    if abs(c) < 1e-12:
        return (-im, re) if s > 0 else (im, -re)
    return re * c - im * s, re * s + im * c


def complex_sum(values, sign):
    count = len(values)
    if count == 1:
        return values
    half = count // 2
    plus = [(a[0] + b[0], a[1] + b[1]) for a, b in zip(values[:half], values[half:])]
    minus = [(a[0] - b[0], a[1] - b[1]) for a, b in zip(values[:half], values[half:])]
    minus = [rotate(z, sign * 2 * math.pi * n / count) for n, z in enumerate(minus)]
    even, odd = complex_sum(plus, sign), complex_sum(minus, sign)
    return [z for pair in zip(even, odd) for z in pair]


def odd_frequencies(values):
    count = len(values)
    if count == 1:
        return {1: (values[0], None)}
    half = count // 2
    joined = [rotate((values[n], -values[n + half]), -math.pi * n / count) for n in range(half)]
    out = {}
    for t, (re, im) in enumerate(complex_sum(joined, -1)):
        k = 4 * t + 1
        if k <= count:
            out[k] = (re, im)
        else:
            out[2 * count - k] = (re, -im)
    return out


def real_transform(values):
    count = len(values)
    if count == 1:
        return {0: (values[0], None)}
    half = count // 2
    even = real_transform([values[n] + values[n + half] for n in range(half)])
    out = {2 * k: z for k, z in even.items()}
    out.update(odd_frequencies([values[n] - values[n + half] for n in range(half)]))
    return out


def padded_transform(values):
    out = {2 * k: z for k, z in real_transform(values).items()}
    out.update(odd_frequencies(values))
    return out


def odd_inverse(terms, count):
    if count == 1:
        return [terms[1][0]]
    half = count // 2
    joined = []
    for t in range(half):
        k = 4 * t + 1
        if k <= count:
            joined.append(terms[k])
        else:
            re, im = terms[2 * count - k]
            joined.append((re, -im))
    turned = [rotate(z, math.pi * n / count) for n, z in enumerate(complex_sum(joined, 1))]
    return [z[0] for z in turned] + [-z[1] for z in turned]


def real_inverse(terms, count):
    if count == 1:
        return [terms[0][0]]
    half = count // 2
    even = real_inverse({k // 2: z for k, z in terms.items() if k % 2 == 0}, half)
    odd = odd_inverse({k: z for k, z in terms.items() if k % 2}, half)
    return [a + b for a, b in zip(even, odd)] + [a - b for a, b in zip(even, odd)]


def padded_inverse(terms, count):
    even = real_inverse({k // 2: z for k, z in terms.items() if k % 2 == 0}, count)
    odd = odd_inverse({k: z for k, z in terms.items() if k % 2}, count)
    return [a + b for a, b in zip(even, odd)]


def split(value):
    high = value.astype(bf16)
    return high, (value - high.astype(f32)).astype(bf16)


def np_split(table):
    table = jnp.asarray(table.astype(np.float32))
    high = table.astype(bf16)
    return high, (table - high.astype(f32)).astype(bf16)


def tables(lat_count, lon_count):
    length = 2 * lat_count
    blocks = lat_count // LANES
    ring = 2 * blocks
    kept = length // 3
    reach = kept // ring + 1
    lane = np.arange(LANES)
    shift = np.where(lane < 2 * reach, lane - reach, 0)
    valid = (lane < 2 * reach).astype(np.float64)
    psi = 2 * np.pi * (lane[:, None] + 0.5) * shift[None, :] / LANES
    cos, sin = np.cos(psi) * valid, np.sin(psi) * valid
    forward = np.block([[cos, sin], [sin, -cos]])
    inverse = np.block([[cos.T, sin.T], [sin.T, -cos.T]])
    small = np.arange(blocks + 1)
    phi = 2 * np.pi * small[:, None] * (lane[None, :] + 0.5) / length
    twist = np.concatenate([np.cos(phi), np.sin(phi)], 1)
    index = small[:, None] + ring * shift[None, :]
    weight = np.where((small == 0) | (small == blocks), 1.0, 2.0)[:, None] / length
    weight = weight * (np.abs(index) <= kept) * valid
    slope = weight * 2 * np.pi * index / length
    factor = np.concatenate([weight, weight, slope, -slope], 1)
    latitude = (np.arange(lat_count) + 0.5) * (np.pi / lat_count) - 0.5 * np.pi
    secant = 1.0 / np.maximum(np.cos(latitude), cos_floor)
    line = np.zeros((8, lat_count))
    line[0] = secant / 60.0
    line[1] = coriolis * np.sin(latitude)
    fields = 3
    own = np.zeros((fields * lon_count, fields * lon_count))
    outer = np.zeros((fields * lon_count, 2 * fields * ROWS))
    for f in range(fields):
        for row in range(lon_count):
            for offset, value in ((1, 45.0), (2, -9.0), (3, 1.0)):
                for sign in (1, -1):
                    at = row + sign * offset
                    if at < 0:
                        outer[f * lon_count + row, f * ROWS + at + ROWS] = sign * value
                    elif at >= lon_count:
                        outer[f * lon_count + row, (fields + f) * ROWS + at - lon_count] = sign * value
                    else:
                        own[f * lon_count + row, f * lon_count + at] = sign * value
    own = np.concatenate([own, own], 1)
    outer = np.concatenate([outer, outer], 1)
    return (
        *np_split(forward),
        *np_split(inverse),
        jnp.asarray(twist.astype(np.float32)),
        jnp.asarray(factor.astype(np.float32)),
        jnp.asarray(line.astype(np.float32)),
        jnp.asarray(own.astype(np.float32)).astype(bf16),
        jnp.asarray(outer.astype(np.float32)).astype(bf16),
    )


def kernel(
    sizes, const_shapes, thick_ref, wind_ref, *refs,
):
    count = len(const_shapes)
    const_hbm, (out_h, out_w), scratch = refs[:count], refs[count : count + 2], refs[count + 2 :]
    const_refs, scratch = scratch[:count], scratch[count:]
    fwd_hi, fwd_lo, inv_hi, inv_lo, twist_ref, factor_ref, line_ref, own_ref, outer_ref = const_refs
    (
        state, opposite, halo, levels, spec_in, gain_own, turned, zonal, smooth, slope, load_sem, const_sem,
        anti_send, anti_recv, halo_send, halo_recv, lev_send, lev_recv,
    ) = scratch
    lon_size, lev_size = sizes
    fields, lon_count, lat_count = state.shape[1:]
    blocks = lat_count // LANES
    groups = lon_count // ROWS
    half = lon_size // 2
    lon, lev = lax.axis_index("lon"), lax.axis_index("lev")
    place = lax.rem(lon, half)
    base = lon - place
    right = base + lax.rem(place + 1, half)
    left = base + lax.rem(place + half - 1, half)
    partner = lax.rem(lon + half, lon_size)
    at_end, at_start = place == half - 1, place == 0
    not_end, not_start = place < half - 1, place > 0
    flip = at_end.astype(jnp.int32)
    has_below, has_above = lev > 0, lev < lev_size - 1

    loads = [pltpu.make_async_copy(thick_ref.at[0], state.at[0, 0], load_sem.at[0])]
    loads += [pltpu.make_async_copy(wind_ref.at[f, 0], state.at[0, f + 1], load_sem.at[f + 1]) for f in range(2)]
    loads += [pltpu.make_async_copy(const_hbm[n], const_refs[n], const_sem.at[n]) for n in range(count)]
    halo[...] = jnp.zeros_like(halo)

    @pl.when(jnp.logical_not(has_below))
    def _():
        for s in range(STEPS):
            levels[s, 0] = jnp.zeros_like(levels[s, 0])

    @pl.when(jnp.logical_not(has_above))
    def _():
        for s in range(STEPS):
            levels[s, 1] = jnp.zeros_like(levels[s, 1])

    barrier = pltpu.get_barrier_semaphore()
    for at in (partner, left, right):
        pl.semaphore_signal(barrier, inc=1, device_id={"lon": at}, device_id_type=MESH)

    @pl.when(has_below)
    def _():
        pl.semaphore_signal(barrier, inc=1, device_id={"lev": lev - 1}, device_id_type=MESH)

    @pl.when(has_above)
    def _():
        pl.semaphore_signal(barrier, inc=1, device_id={"lev": lev + 1}, device_id_type=MESH)

    for copy in loads:
        copy.start()
    pl.semaphore_wait(barrier, 3 + has_below.astype(jnp.int32) + has_above.astype(jnp.int32))

    def rows(g):
        index = g + flip * (groups - 1 - 2 * g)
        return pl.ds(pl.multiple_of(index * ROWS, ROWS), ROWS)

    def source(s, f, at):
        if s == 0:
            return thick_ref.at[0, at] if f == 0 else wind_ref.at[f - 1, 0, at]
        return state.at[s, f, at]

    def anti_copy(s, g, f):
        return pltpu.make_async_remote_copy(
            src_ref=source(s, f, rows(g)), dst_ref=opposite.at[s, f, rows(g)],
            send_sem=anti_send.at[s, g, f], recv_sem=anti_recv.at[s, g, f],
            device_id={"lon": partner}, device_id_type=MESH,
        )

    def halo_copy(s, side, f, relay=False):
        at = pl.ds(lon_count - 3 if side == 0 else 0, 3)
        landing = ROWS - 3 if side == 0 else 0
        return pltpu.make_async_remote_copy(
            src_ref=opposite.at[s, f, at] if relay else source(s, f, at),
            dst_ref=halo.at[s, side, f, pl.ds(landing, 3)],
            send_sem=halo_send.at[s, side, f], recv_sem=halo_recv.at[s, side, f],
            device_id={"lon": right if side == 0 else left}, device_id_type=MESH,
        )

    def lev_copy(s, g, side):
        return pltpu.make_async_remote_copy(
            src_ref=source(s, 0, rows(g)), dst_ref=levels.at[s, side, rows(g)],
            send_sem=lev_send.at[s, g, side], recv_sem=lev_recv.at[s, g, side],
            device_id={"lev": lev + 1 if side == 0 else lev - 1}, device_id_type=MESH,
        )

    def send_halo(s):
        for side, inner in ((0, not_end), (1, not_start)):

            @pl.when(inner)
            def _(side=side):
                for f in range(fields):
                    halo_copy(s, side, f).start()

    def relay_halo(s):
        for side, outer in ((0, at_end), (1, at_start)):

            @pl.when(outer)
            def _(side=side):
                for f in range(fields):
                    halo_copy(s, side, f, True).start()

    def send_group(s, g):
        for f in range(fields):
            anti_copy(s, g, f).start()

        @pl.when(has_above)
        def _():
            lev_copy(s, g, 0).start()

        @pl.when(has_below)
        def _():
            lev_copy(s, g, 1).start()

    def product(value, high, low):
        top, rest = split(value)
        out = jnp.dot(top, low[...], preferred_element_type=f32)
        out += jnp.dot(rest, high[...], preferred_element_type=f32)
        return out + jnp.dot(top, high[...], preferred_element_type=f32)

    def transform_half(ref, s, g, f):
        values = [ref[s, f, rows(g), n * LANES : (n + 1) * LANES] for n in range(blocks)]
        for k, (re, im) in padded_transform(values).items():
            at = k * ROWS
            c, d = twist_ref[k : k + 1, :LANES], twist_ref[k : k + 1, LANES:]
            if k == 0:
                out = (re, jnp.zeros_like(re))
            elif im is None:
                out = (re * c, -re * d)
            else:
                out = (re * c + im * d, im * c - re * d)
            spec_in[at : at + ROWS, :LANES] = out[0]
            spec_in[at : at + ROWS, LANES:] = out[1]
        return product(spec_in[...], fwd_hi, fwd_lo)

    def own_group(s, g):
        for f in range(fields):
            gain_own[g, f] = transform_half(state, s, g, f)

    def own_zonal(s):
        value = state[s].reshape(fields * lon_count, lat_count)
        zonal[...] = jnp.dot(own_ref[...], jnp.concatenate(split(value), 0), preferred_element_type=f32)

    def outer_zonal(s):
        for side in range(2):
            for f in range(fields):
                halo_copy(s, side, f).wait_recv()
        value = halo[s].reshape(2 * fields * ROWS, lat_count)
        zonal[...] += jnp.dot(outer_ref[...], jnp.concatenate(split(value), 0), preferred_element_type=f32)

    spectral = (blocks + 1) * ROWS

    def back(f, which):
        target = smooth if which == 0 else slope
        terms = {}
        for k in range(blocks + 1):
            at = which * spectral + k * ROWS
            re, im = turned[at : at + ROWS, :LANES], turned[at : at + ROWS, LANES:]
            c, d = twist_ref[k : k + 1, :LANES], twist_ref[k : k + 1, LANES:]
            if k == 0:
                terms[k] = (re, None)
            elif k == blocks:
                terms[k] = (re * c - im * d, None)
            else:
                terms[k] = (re * c - im * d, re * d + im * c)
        for n, value in enumerate(padded_inverse(terms, blocks)):
            target[f, :, n * LANES : (n + 1) * LANES] = value

    def group(s, g):
        for f in range(fields):
            anti_copy(s, g, f).wait_recv()
            if g == 0 and f == fields - 1:
                relay_halo(s)
            theirs = transform_half(opposite, s, g, f)
            mine = gain_own[g, f]
            sign = 1.0 if f == 0 else -1.0
            for k in range(blocks + 1):
                at = k * ROWS
                a = mine[at : at + ROWS, :LANES] + sign * theirs[at : at + ROWS, :LANES]
                b = mine[at : at + ROWS, LANES:] - sign * theirs[at : at + ROWS, LANES:]
                w = factor_ref[k : k + 1]
                turned[at : at + ROWS, :LANES] = a * w[:, :LANES]
                turned[at : at + ROWS, LANES:] = b * w[:, LANES : 2 * LANES]
                at += spectral
                turned[at : at + ROWS, :LANES] = b * w[:, 2 * LANES : 3 * LANES]
                turned[at : at + ROWS, LANES:] = a * w[:, 3 * LANES :]
            turned[...] = product(turned[...], inv_hi, inv_lo)
            for which in range(2):
                back(f, which)
        if g == 0:
            outer_zonal(s)

        @pl.when(has_below)
        def _():
            lev_copy(s, g, 0).wait_recv()

        @pl.when(has_above)
        def _():
            lev_copy(s, g, 1).wait_recv()

        r = rows(g)
        for n in range(blocks):
            lanes = slice(n * LANES, (n + 1) * LANES)
            h, u, v = (state[s, f, r, lanes] for f in range(fields))
            secant, turn = line_ref[0:1, lanes], line_ref[1:2, lanes]
            zh, zu, zv = (zonal[pl.ds(f * lon_count + r.start, ROWS), lanes] * secant for f in range(fields))
            mh, mu, mv = (slope[f, :, lanes] for f in range(fields))
            vertical = levels[s, 0, r, lanes] + levels[s, 1, r, lanes] - 2.0 * h
            th = mixing * vertical - (u * zh + v * mh) - h * (zu + mv)
            tu = turn * v - (u * zu + v * mu) - zh
            tv = -(u * zv + v * mv) - mh - turn * u
            nh, nu, nv = (smooth[f, :, lanes] + courant * t for f, t in enumerate((th, tu, tv)))
            if s < STEPS - 1:
                state[s + 1, 0, r, lanes] = nh
                state[s + 1, 1, r, lanes] = nu
                state[s + 1, 2, r, lanes] = nv
            else:
                out_h[0, r, lanes] = nh
                out_w[0, 0, r, lanes] = nu
                out_w[1, 0, r, lanes] = nv

    for g in range(groups):
        send_group(0, g)
        if g == 0:
            send_halo(0)
    for copy in loads:
        copy.wait()
    for g in range(groups):
        own_group(0, g)
    for s in range(STEPS):
        own_zonal(s)
        for g in range(groups):
            group(s, g)
            if s < STEPS - 1:
                send_group(s + 1, g)
                if g == groups - 1:
                    send_halo(s + 1)
                own_group(s + 1, g)
    for s in range(STEPS):
        for g in range(groups):
            for f in range(fields):
                anti_copy(s, g, f).wait_send()

            @pl.when(has_above)
            def _():
                lev_copy(s, g, 0).wait_send()

            @pl.when(has_below)
            def _():
                lev_copy(s, g, 1).wait_send()

        for side in range(2):
            for f in range(fields):
                halo_copy(s, side, f).wait_send()


def body(sizes, thickness, wind_field):
    level_count, lon_count, lat_count = thickness.shape
    fields = 3
    groups = lon_count // ROWS
    blocks = lat_count // LANES
    spectral = (blocks + 1) * ROWS
    consts = tables(lat_count, lon_count)
    vmem = pl.BlockSpec(memory_space=pltpu.VMEM)
    hbm = pl.BlockSpec(memory_space=pltpu.HBM)
    dma = pltpu.SemaphoreType.DMA
    return pl.pallas_call(
        functools.partial(kernel, sizes, [c.shape for c in consts]),
        out_shape=(
            jax.ShapeDtypeStruct(thickness.shape, f32),
            jax.ShapeDtypeStruct(wind_field.shape, f32),
        ),
        in_specs=[hbm, hbm] + [hbm] * len(consts),
        out_specs=(vmem, vmem),
        scratch_shapes=[pltpu.VMEM(c.shape, c.dtype) for c in consts]
        + [
            pltpu.VMEM((STEPS, fields, lon_count, lat_count), f32),
            pltpu.VMEM((STEPS, fields, lon_count, lat_count), f32),
            pltpu.VMEM((STEPS, 2, fields, ROWS, lat_count), f32),
            pltpu.VMEM((STEPS, 2, lon_count, lat_count), f32),
            pltpu.VMEM((spectral, 2 * LANES), f32),
            pltpu.VMEM((groups, fields, spectral, 2 * LANES), f32),
            pltpu.VMEM((2 * spectral, 2 * LANES), f32),
            pltpu.VMEM((fields * lon_count, lat_count), f32),
            pltpu.VMEM((fields, ROWS, lat_count), f32),
            pltpu.VMEM((fields, ROWS, lat_count), f32),
            dma((fields,)),
            dma((len(consts),)),
            dma((STEPS, groups, fields)),
            dma((STEPS, groups, fields)),
            dma((STEPS, 2, fields)),
            dma((STEPS, 2, fields)),
            dma((STEPS, groups, 2)),
            dma((STEPS, groups, 2)),
        ],
        name="sphere_steps",
        compiler_params=pltpu.CompilerParams(collective_id=0, has_side_effects=True, vmem_limit_bytes=67_043_328),
    )(thickness, wind_field, *consts)


def solution(mesh):
    sizes = (mesh.shape["lon"], mesh.shape["lev"])
    in_specs = (P("lev", "lon", None), P(None, "lev", "lon", None))
    out_specs = (P("lev", "lon", None), P(None, "lev", "lon", None))
    return jax.shard_map(
        functools.partial(body, sizes), mesh=mesh, in_specs=in_specs, out_specs=out_specs, check_vma=False
    )
```

```python
import functools
import math

import jax
import jax.numpy as jnp
import numpy as np
from jax import lax
from jax.experimental import pallas as pl
from jax.experimental.pallas import tpu as pltpu
from jax.sharding import PartitionSpec as P

STEPS = 2
MESH = pl.DeviceIdType.MESH

courant = 0.2
mixing = 0.25
coriolis = 0.5
cos_floor = 0.25

LANES = 128
ROWS = 8
f32 = jnp.float32
bf16 = jnp.bfloat16


def rotate(z, angle):
    re, im = z
    c, s = math.cos(angle), math.sin(angle)
    if abs(s) < 1e-12:
        return (re, im) if c > 0 else (-re, -im)
    if abs(c) < 1e-12:
        return (-im, re) if s > 0 else (im, -re)
    return re * c - im * s, re * s + im * c


def complex_sum(values, sign):
    count = len(values)
    if count == 1:
        return values
    half = count // 2
    plus = [(a[0] + b[0], a[1] + b[1]) for a, b in zip(values[:half], values[half:])]
    minus = [(a[0] - b[0], a[1] - b[1]) for a, b in zip(values[:half], values[half:])]
    minus = [rotate(z, sign * 2 * math.pi * n / count) for n, z in enumerate(minus)]
    even, odd = complex_sum(plus, sign), complex_sum(minus, sign)
    return [z for pair in zip(even, odd) for z in pair]


def odd_frequencies(values):
    count = len(values)
    if count == 1:
        return {1: (values[0], None)}
    half = count // 2
    joined = [rotate((values[n], -values[n + half]), -math.pi * n / count) for n in range(half)]
    out = {}
    for t, (re, im) in enumerate(complex_sum(joined, -1)):
        k = 4 * t + 1
        if k <= count:
            out[k] = (re, im)
        else:
            out[2 * count - k] = (re, -im)
    return out


def real_transform(values):
    count = len(values)
    if count == 1:
        return {0: (values[0], None)}
    half = count // 2
    even = real_transform([values[n] + values[n + half] for n in range(half)])
    out = {2 * k: z for k, z in even.items()}
    out.update(odd_frequencies([values[n] - values[n + half] for n in range(half)]))
    return out


def padded_transform(values):
    out = {2 * k: z for k, z in real_transform(values).items()}
    out.update(odd_frequencies(values))
    return out


def odd_inverse(terms, count):
    if count == 1:
        return [terms[1][0]]
    half = count // 2
    joined = []
    for t in range(half):
        k = 4 * t + 1
        if k <= count:
            joined.append(terms[k])
        else:
            re, im = terms[2 * count - k]
            joined.append((re, -im))
    turned = [rotate(z, math.pi * n / count) for n, z in enumerate(complex_sum(joined, 1))]
    return [z[0] for z in turned] + [-z[1] for z in turned]


def real_inverse(terms, count):
    if count == 1:
        return [terms[0][0]]
    half = count // 2
    even = real_inverse({k // 2: z for k, z in terms.items() if k % 2 == 0}, half)
    odd = odd_inverse({k: z for k, z in terms.items() if k % 2}, half)
    return [a + b for a, b in zip(even, odd)] + [a - b for a, b in zip(even, odd)]


def padded_inverse(terms, count):
    even = real_inverse({k // 2: z for k, z in terms.items() if k % 2 == 0}, count)
    odd = odd_inverse({k: z for k, z in terms.items() if k % 2}, count)
    return [a + b for a, b in zip(even, odd)]


def split(value):
    high = value.astype(bf16)
    return high, (value - high.astype(f32)).astype(bf16)


def np_split(table):
    table = jnp.asarray(table.astype(np.float32))
    high = table.astype(bf16)
    return high, (table - high.astype(f32)).astype(bf16)


def tables(lat_count):
    length = 2 * lat_count
    blocks = lat_count // LANES
    ring = 2 * blocks
    kept = length // 3
    reach = kept // ring + 1
    lane = np.arange(LANES)
    shift = np.where(lane < 2 * reach, lane - reach, 0)
    valid = (lane < 2 * reach).astype(np.float64)
    psi = 2 * np.pi * (lane[:, None] + 0.5) * shift[None, :] / LANES
    cos, sin = np.cos(psi) * valid, np.sin(psi) * valid
    forward = np.block([[cos, sin], [sin, -cos]])
    inverse = np.block([[cos.T, sin.T], [sin.T, -cos.T]])
    small = np.arange(blocks + 1)
    phi = 2 * np.pi * small[:, None] * (lane[None, :] + 0.5) / length
    twist = np.concatenate([np.cos(phi), np.sin(phi)], 1)
    index = small[:, None] + ring * shift[None, :]
    weight = np.where((small == 0) | (small == blocks), 1.0, 2.0)[:, None] / length
    weight = weight * (np.abs(index) <= kept) * valid
    slope = weight * 2 * np.pi * index / length
    factor = np.concatenate([weight, weight, slope, -slope], 1)
    latitude = (np.arange(lat_count) + 0.5) * (np.pi / lat_count) - 0.5 * np.pi
    secant = 1.0 / np.maximum(np.cos(latitude), cos_floor)
    line = np.zeros((8, lat_count))
    line[0] = secant / 60.0
    line[1] = coriolis * np.sin(latitude)
    parts = 2 * 3
    own = np.zeros((parts * ROWS, parts * ROWS))
    outer = np.zeros((parts * ROWS, parts * ROWS))
    for part in range(parts):
        for row in range(ROWS):
            for offset, value in ((1, 45.0), (2, -9.0), (3, 1.0)):
                for sign in (1, -1):
                    at = row + sign * offset
                    target = own if 0 <= at < ROWS else outer
                    target[part * ROWS + row, part * ROWS + at % ROWS] = sign * value
    own = np.concatenate([own, own], 1)
    outer = np.concatenate([outer, outer], 1)
    return (
        *np_split(forward),
        *np_split(inverse),
        jnp.asarray(twist.astype(np.float32)),
        jnp.asarray(factor.astype(np.float32)),
        jnp.asarray(line.astype(np.float32)),
        jnp.asarray(own.astype(np.float32)).astype(bf16),
        jnp.asarray(outer.astype(np.float32)).astype(bf16),
    )


def kernel(sizes, const_shapes, thick_ref, wind_ref, *refs):
    count = len(const_shapes)
    const_hbm, (out_h, out_w), scratch = refs[:count], refs[count : count + 2], refs[count + 2 :]
    const_refs, scratch = scratch[:count], scratch[count:]
    fwd_hi, fwd_lo, inv_hi, inv_lo, twist_ref, factor_ref, line_ref, own_ref, outer_ref = const_refs
    (
        state, halo, far, levels, spec_in, turned, zonal, smooth, slope, redo, const_sem, first_send, first_recv,
        far_send, far_recv, halo_send, halo_recv, lev_send, lev_recv, last_send, last_recv,
    ) = scratch
    lon_size, lev_size = sizes
    fields, _, lat_count = state.shape[1:]
    blocks = lat_count // LANES
    half = lon_size // 2
    chips = half // 2
    depth = 2 * lev_size
    lon, lev = lax.axis_index("lon"), lax.axis_index("lev")
    side_now = lon // half
    chip = (lon % half) // 2
    core = lon % 2
    odd = chip % 2
    z = side_now * lev_size + lev

    there = (z + lev_size // 2 + lev_size * ((odd + core + side_now) % 2)) % depth

    def owner(q):
        return {"lon": (there // lev_size) * half + 2 * chip + q, "lev": there % lev_size}

    place = (z + depth - lev_size // 2) % depth
    level = place % lev_size
    held_by = (place // lev_size + odd) % 2

    def holder(hemi):
        return {"lon": hemi * half + 2 * chip + held_by, "lev": level}

    across = (1 - side_now) * half + 2 * chip
    after = side_now * half + 2 * ((chip + 1) % chips)
    before = side_now * half + 2 * ((chip + chips - 1) % chips) + 1
    right = (1 - core) * (lon + 1) + core * ((1 - held_by) * across + held_by * after)
    left = core * (lon - 1) + (1 - core) * (held_by * (across + 1) + (1 - held_by) * before)
    swap_right = core * held_by * (chip // (chips - 1))
    swap_left = (1 - core) * (1 - held_by) * ((chips - 1 - chip) // (chips - 1))
    has_below, has_above = level > 0, level < lev_size - 1
    far_right, far_left = core * (1 - held_by), (1 - core) * held_by
    crossing = far_right + far_left
    beyond = (there + lev_size) % depth
    far_owner = {"lon": (beyond // lev_size) * half + 2 * chip + core, "lev": beyond % lev_size}

    def far_holder(hemi):
        return {"lon": hemi * half + 2 * chip + 1 - held_by, "lev": level}

    def at_height(height):
        return {"lon": (height // lev_size) * half + 2 * chip + core, "lev": height % lev_size}

    upward, downward = at_height((z + 1) % depth), at_height((z + depth - 1) % depth)

    loads = [pltpu.make_async_copy(const_hbm[n], const_refs[n], const_sem.at[n]) for n in range(count)]
    for copy in loads:
        copy.start()
    halo[...] = jnp.zeros_like(halo)
    far[...] = jnp.zeros_like(far)

    @pl.when(jnp.logical_not(has_below))
    def _():
        for s in range(STEPS):
            levels[s, 0] = jnp.zeros_like(levels[s, 0])

    @pl.when(jnp.logical_not(has_above))
    def _():
        for s in range(STEPS):
            levels[s, 1] = jnp.zeros_like(levels[s, 1])

    barrier = pltpu.get_barrier_semaphore()
    for device in (owner(0), owner(1), holder(0), holder(1), far_owner, {"lon": left}, {"lon": right}):
        pl.semaphore_signal(barrier, inc=1, device_id=device, device_id_type=MESH)

    @pl.when(crossing > 0)
    def _():
        for hemi in range(2):
            pl.semaphore_signal(barrier, inc=1, device_id=far_holder(hemi), device_id_type=MESH)

    @pl.when(has_below)
    def _():
        pl.semaphore_signal(barrier, inc=1, device_id=downward, device_id_type=MESH)

    @pl.when(has_above)
    def _():
        pl.semaphore_signal(barrier, inc=1, device_id=upward, device_id_type=MESH)

    def rows(part):
        return pl.ds(pl.multiple_of(part * ROWS, ROWS), ROWS)

    def first_copy(q, f, hemi):
        at = rows(q)
        return pltpu.make_async_remote_copy(
            src_ref=thick_ref.at[0, at] if f == 0 else wind_ref.at[f - 1, 0, at], dst_ref=state.at[0, f, rows(hemi)],
            send_sem=first_send.at[q, f], recv_sem=first_recv.at[hemi, f],
            device_id=owner(q), device_id_type=MESH,
        )

    def early_far_copy(f, side, hemi):
        at = pl.ds(2 * ROWS - 3 if side == 0 else 0, 3)
        return pltpu.make_async_remote_copy(
            src_ref=thick_ref.at[0, at] if f == 0 else wind_ref.at[f - 1, 0, at],
            dst_ref=far.at[0, f, hemi, pl.ds(ROWS - 3 if side == 0 else 0, 3)],
            send_sem=far_send.at[0, f, 0], recv_sem=far_recv.at[0, f, hemi],
            device_id=far_owner, device_id_type=MESH,
        )

    def last_copy(part, f, hemi, q, origin, span):
        start, length = span
        source = origin.at[f, pl.ds(hemi * ROWS + start, length)]
        at = pl.ds(q * ROWS + start, length)
        return pltpu.make_async_remote_copy(
            src_ref=source, dst_ref=out_h.at[0, at] if f == 0 else out_w.at[f - 1, 0, at],
            send_sem=last_send.at[part, hemi, f], recv_sem=last_recv.at[part, q, f],
            device_id=holder(hemi), device_id_type=MESH,
        )

    def halo_copy(s, side, f, hemi, distant=False):
        start = ROWS - 3 if side == 0 else 0
        to = hemi if distant else (hemi + (swap_right if side == 0 else swap_left)) % 2
        send, recv = far_send.at[s, f, hemi], far_recv.at[s, f, hemi]
        if not distant:
            send, recv = halo_send.at[s, side, f, hemi], halo_recv.at[s, side, f, to]
        return pltpu.make_async_remote_copy(
            src_ref=state.at[s, f, pl.ds(hemi * ROWS + start, 3)],
            dst_ref=(far if distant else halo).at[s, f, to, pl.ds(start, 3)],
            send_sem=send, recv_sem=recv,
            device_id={"lon": right if side == 0 else left}, device_id_type=MESH,
        )

    def lev_copy(s, side, hemi):
        return pltpu.make_async_remote_copy(
            src_ref=state.at[s, 0, rows(hemi)], dst_ref=levels.at[s, side, rows(hemi)],
            send_sem=lev_send.at[s, side, hemi], recv_sem=lev_recv.at[s, side, hemi],
            device_id=upward if side == 0 else downward, device_id_type=MESH,
        )

    whole, spans = (0, ROWS), {0: ((0, ROWS - 3), (ROWS - 3, 3)), 1: ((3, ROWS - 3), (0, 3))}

    def if_far(action):
        for side, flag in ((0, far_right), (1, far_left)):

            @pl.when(flag > 0)
            def _(side=side):
                action(side)

    def send_halo(s, hemi, chosen):
        def distant(side):
            for f in chosen:
                halo_copy(s, side, f, hemi, True).start()

        if s > 0:
            if_far(distant)
        for side, flag in ((0, far_right), (1, far_left)):

            @pl.when(flag == 0)
            def _(side=side):
                for f in chosen:
                    halo_copy(s, side, f, hemi).start()

    def near_halo(s, wait):
        for side, flag in ((0, far_left), (1, far_right)) if wait == "wait_recv" else ((0, far_right), (1, far_left)):

            @pl.when(flag == 0)
            def _(side=side):
                for f in range(fields):
                    for hemi in range(2):
                        getattr(halo_copy(s, side, f, hemi), wait)()

    def far_wait(s):
        for f in range(fields):
            for hemi in range(2):
                halo_copy(s, 1, f, hemi, True).wait_recv()

    def each_level(s, hemi, action):
        for side, flags in ((0, (has_above, has_below)), (1, (has_below, has_above))):

            @pl.when(flags[1 if action == "wait_recv" else 0])
            def _(side=side):
                getattr(lev_copy(s, side, hemi), action)()

    def product(value, high, low):
        top, rest = split(value)
        out = jnp.dot(top, low[...], preferred_element_type=f32)
        out += jnp.dot(rest, high[...], preferred_element_type=f32)
        return out + jnp.dot(top, high[...], preferred_element_type=f32)

    spectral = (blocks + 1) * 2 * ROWS

    def spectra(s, f):
        for hemi in range(2):
            r = slice(hemi * ROWS, (hemi + 1) * ROWS)
            values = [state[s, f, r, n * LANES : (n + 1) * LANES] for n in range(blocks)]
            for k, (re, im) in padded_transform(values).items():
                at = (2 * k + hemi) * ROWS
                c, d = twist_ref[k : k + 1, :LANES], twist_ref[k : k + 1, LANES:]
                if k == 0:
                    out = (re, jnp.zeros_like(re))
                elif im is None:
                    out = (re * c, -re * d)
                else:
                    out = (re * c + im * d, im * c - re * d)
                spec_in[at : at + ROWS, :LANES] = out[0]
                spec_in[at : at + ROWS, LANES:] = out[1]
        gains = product(spec_in[...], fwd_hi, fwd_lo)
        sign = 1.0 if f == 0 else -1.0
        for k in range(blocks + 1):
            at = 2 * k * ROWS
            to = at + ROWS
            end = to + ROWS
            a = gains[at:to, :LANES] + sign * gains[to:end, :LANES]
            b = gains[at:to, LANES:] - sign * gains[to:end, LANES:]
            w = factor_ref[k : k + 1]
            pieces = (a * w[:, :LANES], b * w[:, LANES : 2 * LANES])
            turned[at:to, :LANES] = pieces[0]
            turned[at:to, LANES:] = pieces[1]
            turned[to:end, :LANES] = sign * pieces[0]
            turned[to:end, LANES:] = -sign * pieces[1]
            at, to, end = at + spectral, to + spectral, end + spectral
            pieces = (b * w[:, 2 * LANES : 3 * LANES], a * w[:, 3 * LANES :])
            turned[at:to, :LANES] = pieces[0]
            turned[at:to, LANES:] = pieces[1]
            turned[to:end, :LANES] = -sign * pieces[0]
            turned[to:end, LANES:] = sign * pieces[1]
        turned[...] = product(turned[...], inv_hi, inv_lo)
        for which, target in enumerate((smooth, slope)):
            for hemi in range(2):
                terms = {}
                for k in range(blocks + 1):
                    at = which * spectral + (2 * k + hemi) * ROWS
                    re, im = turned[at : at + ROWS, :LANES], turned[at : at + ROWS, LANES:]
                    c, d = twist_ref[k : k + 1, :LANES], twist_ref[k : k + 1, LANES:]
                    if k == 0:
                        terms[k] = (re, None)
                    elif k == blocks:
                        terms[k] = (re * c - im * d, None)
                    else:
                        terms[k] = (re * c - im * d, re * d + im * c)
                r = slice(hemi * ROWS, (hemi + 1) * ROWS)
                for n, value in enumerate(padded_inverse(terms, blocks)):
                    target[f, r, n * LANES : (n + 1) * LANES] = value

    def own_zonal(s):
        value = state[s].reshape(fields * 2 * ROWS, lat_count)
        zonal[...] = jnp.dot(own_ref[...], jnp.concatenate(split(value), 0), preferred_element_type=f32)

    def outer_zonal(value):
        value = value.reshape(fields * 2 * ROWS, lat_count)
        zonal[...] += jnp.dot(outer_ref[...], jnp.concatenate(split(value), 0), preferred_element_type=f32)

    def advance(s, hemi, target):
        r = slice(hemi * ROWS, (hemi + 1) * ROWS)
        for n in range(blocks):
            lanes = slice(n * LANES, (n + 1) * LANES)
            h, u, v = (state[s, f, r, lanes] for f in range(fields))
            secant, turn = line_ref[0:1, lanes], line_ref[1:2, lanes]
            zh, zu, zv = (
                zonal[(2 * f + hemi) * ROWS : (2 * f + hemi + 1) * ROWS, lanes] * secant for f in range(fields)
            )
            mh, mu, mv = (slope[f, r, lanes] for f in range(fields))
            vertical = levels[s, 0, r, lanes] + levels[s, 1, r, lanes] - 2.0 * h
            th = mixing * vertical - (u * zh + v * mh) - h * (zu + mv)
            tu = turn * v - (u * zu + v * mu) - zh
            tv = -(u * zv + v * mv) - mh - turn * u
            for f, t in enumerate((th, tu, tv)):
                target[f, r, lanes] = smooth[f, r, lanes] + courant * t

    count_here = 7 + 2 * crossing + has_below.astype(jnp.int32) + has_above.astype(jnp.int32)
    pl.semaphore_wait(barrier, count_here)
    for f in range(fields):
        for q in range(2):
            first_copy(q, f, side_now).start()
        for side in range(2):

            @pl.when(core == side)
            def _(side=side):
                early_far_copy(f, side, side_now).start()

    for copy in loads:
        copy.wait()
    for s in range(STEPS):
        for f in range(fields):
            if s == 0:
                for hemi in range(2):
                    first_copy(core, f, hemi).wait_recv()
                    if f == 0:
                        each_level(0, hemi, "start")
                    send_halo(0, hemi, (f,))
            spectra(s, f)
        own_zonal(s)
        near_halo(s, "wait_recv")
        if s < STEPS - 1:

            @pl.when(crossing > 0)
            def _():
                far_wait(s)

            outer_zonal(halo[s] + far[s])
        else:
            outer_zonal(halo[s])
        for hemi in range(2):
            each_level(s, hemi, "wait_recv")
            target = state.at[s + 1]
            advance(s, hemi, target)
            if s < STEPS - 1:
                send_halo(s + 1, hemi, range(fields))
                each_level(s + 1, hemi, "start")
                continue

            @pl.when(crossing == 0)
            def _(hemi=hemi):
                for f in range(fields):
                    last_copy(0, f, hemi, core, target, whole).start()

            @if_far
            def _(side, hemi=hemi):
                for f in range(fields):
                    last_copy(0, f, hemi, 1 - side, target, spans[side][0]).start()

    @pl.when(crossing > 0)
    def _():
        far_wait(STEPS - 1)
        outer_zonal(far[STEPS - 1])
        for hemi in range(2):
            advance(STEPS - 1, hemi, redo)

            @if_far
            def _(side, hemi=hemi):
                for f in range(fields):
                    last_copy(1, f, hemi, 1 - side, redo, spans[side][1]).start()

    target = state.at[STEPS]
    for side in range(2):

        @pl.when(core == side)
        def _(side=side):
            for f in range(fields):
                last_copy(0, f, 0, side, target, whole).wait_recv()
                last_copy(0, f, 0, 1 - side, target, spans[side][0]).wait_recv()
                last_copy(1, f, 0, 1 - side, redo, spans[side][1]).wait_recv()

    for f in range(fields):
        for q in range(2):
            first_copy(q, f, side_now).wait_send()
        early_far_copy(f, 0, side_now).wait_send()
    for hemi in range(2):

        @pl.when(crossing == 0)
        def _(hemi=hemi):
            for f in range(fields):
                last_copy(0, f, hemi, core, target, whole).wait_send()

        @if_far
        def _(side, hemi=hemi):
            for f in range(fields):
                for s in range(1, STEPS):
                    halo_copy(s, side, f, hemi, True).wait_send()
                last_copy(0, f, hemi, 1 - side, target, spans[side][0]).wait_send()
                last_copy(1, f, hemi, 1 - side, redo, spans[side][1]).wait_send()

        for s in range(STEPS):
            each_level(s, hemi, "wait_send")
    for s in range(STEPS):
        near_halo(s, "wait_send")


def body(sizes, thickness, wind_field):
    level_count, lon_count, lat_count = thickness.shape
    fields = 3
    blocks = lat_count // LANES
    spectral = (blocks + 1) * 2 * ROWS
    consts = tables(lat_count)
    hbm = pl.BlockSpec(memory_space=pltpu.HBM)
    dma = pltpu.SemaphoreType.DMA
    return pl.pallas_call(
        functools.partial(kernel, sizes, [c.shape for c in consts]),
        out_shape=(
            jax.ShapeDtypeStruct(thickness.shape, f32),
            jax.ShapeDtypeStruct(wind_field.shape, f32),
        ),
        in_specs=[hbm, hbm] + [hbm] * len(consts),
        out_specs=(hbm, hbm),
        scratch_shapes=[pltpu.VMEM(c.shape, c.dtype) for c in consts]
        + [
            pltpu.VMEM((STEPS + 1, fields, lon_count, lat_count), f32),
            pltpu.VMEM((STEPS, fields, 2, ROWS, lat_count), f32),
            pltpu.VMEM((STEPS, fields, 2, ROWS, lat_count), f32),
            pltpu.VMEM((STEPS, 2, lon_count, lat_count), f32),
            pltpu.VMEM((spectral, 2 * LANES), f32),
            pltpu.VMEM((2 * spectral, 2 * LANES), f32),
            pltpu.VMEM((fields * lon_count, lat_count), f32),
            pltpu.VMEM((fields, lon_count, lat_count), f32),
            pltpu.VMEM((fields, lon_count, lat_count), f32),
            pltpu.VMEM((fields, lon_count, lat_count), f32),
            dma((len(consts),)),
            dma((2, fields)),
            dma((2, fields)),
            dma((STEPS, fields, 2)),
            dma((STEPS, fields, 2)),
            dma((STEPS, 2, fields, 2)),
            dma((STEPS, 2, fields, 2)),
            dma((STEPS, 2, 2)),
            dma((STEPS, 2, 2)),
            dma((2, 2, fields)),
            dma((2, 2, fields)),
        ],
        name="sphere_steps",
        compiler_params=pltpu.CompilerParams(collective_id=0, has_side_effects=True, vmem_limit_bytes=67_043_328),
    )(thickness, wind_field, *consts)


def solution(mesh):
    sizes = (mesh.shape["lon"], mesh.shape["lev"])
    in_specs = (P("lev", "lon", None), P(None, "lev", "lon", None))
    out_specs = (P("lev", "lon", None), P(None, "lev", "lon", None))
    return jax.shard_map(
        functools.partial(body, sizes), mesh=mesh, in_specs=in_specs, out_specs=out_specs, check_vma=False
    )
```

```python
import functools
import math

import jax
import jax.numpy as jnp
import numpy as np
from jax import lax
from jax.experimental import pallas as pl
from jax.experimental.pallas import tpu as pltpu
from jax.sharding import PartitionSpec as P

STEPS = 2
MESH = pl.DeviceIdType.MESH

courant = 0.2
mixing = 0.25
coriolis = 0.5
cos_floor = 0.25

LANES = 128
ROWS = 8
f32 = jnp.float32
bf16 = jnp.bfloat16


def rotate(z, angle):
    re, im = z
    c, s = math.cos(angle), math.sin(angle)
    if abs(s) < 1e-12:
        return (re, im) if c > 0 else (-re, -im)
    if abs(c) < 1e-12:
        return (-im, re) if s > 0 else (im, -re)
    return re * c - im * s, re * s + im * c


def complex_sum(values, sign):
    count = len(values)
    if count == 1:
        return values
    half = count // 2
    plus = [(a[0] + b[0], a[1] + b[1]) for a, b in zip(values[:half], values[half:])]
    minus = [(a[0] - b[0], a[1] - b[1]) for a, b in zip(values[:half], values[half:])]
    minus = [rotate(z, sign * 2 * math.pi * n / count) for n, z in enumerate(minus)]
    even, odd = complex_sum(plus, sign), complex_sum(minus, sign)
    return [z for pair in zip(even, odd) for z in pair]


def odd_frequencies(values):
    count = len(values)
    if count == 1:
        return {1: (values[0], None)}
    half = count // 2
    joined = [rotate((values[n], -values[n + half]), -math.pi * n / count) for n in range(half)]
    out = {}
    for t, (re, im) in enumerate(complex_sum(joined, -1)):
        k = 4 * t + 1
        if k <= count:
            out[k] = (re, im)
        else:
            out[2 * count - k] = (re, -im)
    return out


def real_transform(values):
    count = len(values)
    if count == 1:
        return {0: (values[0], None)}
    half = count // 2
    even = real_transform([values[n] + values[n + half] for n in range(half)])
    out = {2 * k: z for k, z in even.items()}
    out.update(odd_frequencies([values[n] - values[n + half] for n in range(half)]))
    return out


def padded_transform(values):
    out = {2 * k: z for k, z in real_transform(values).items()}
    out.update(odd_frequencies(values))
    return out


def odd_inverse(terms, count):
    if count == 1:
        return [terms[1][0]]
    half = count // 2
    joined = []
    for t in range(half):
        k = 4 * t + 1
        if k <= count:
            joined.append(terms[k])
        else:
            re, im = terms[2 * count - k]
            joined.append((re, -im))
    turned = [rotate(z, math.pi * n / count) for n, z in enumerate(complex_sum(joined, 1))]
    return [z[0] for z in turned] + [-z[1] for z in turned]


def real_inverse(terms, count):
    if count == 1:
        return [terms[0][0]]
    half = count // 2
    even = real_inverse({k // 2: z for k, z in terms.items() if k % 2 == 0}, half)
    odd = odd_inverse({k: z for k, z in terms.items() if k % 2}, half)
    return [a + b for a, b in zip(even, odd)] + [a - b for a, b in zip(even, odd)]


def padded_inverse(terms, count):
    even = real_inverse({k // 2: z for k, z in terms.items() if k % 2 == 0}, count)
    odd = odd_inverse({k: z for k, z in terms.items() if k % 2}, count)
    return [a + b for a, b in zip(even, odd)]


def split(value):
    high = value.astype(bf16)
    return high, (value - high.astype(f32)).astype(bf16)


def np_split(table):
    table = jnp.asarray(table.astype(np.float32))
    high = table.astype(bf16)
    return high, (table - high.astype(f32)).astype(bf16)


def tables(lat_count):
    length = 2 * lat_count
    blocks = lat_count // LANES
    ring = 2 * blocks
    kept = length // 3
    reach = kept // ring + 1
    lane = np.arange(LANES)
    shift = np.where(lane < 2 * reach, lane - reach, 0)
    valid = (lane < 2 * reach).astype(np.float64)
    psi = 2 * np.pi * (lane[:, None] + 0.5) * shift[None, :] / LANES
    cos, sin = np.cos(psi) * valid, np.sin(psi) * valid
    forward = np.block([[cos, sin], [sin, -cos]])
    inverse = np.block([[cos.T, sin.T], [sin.T, -cos.T]])
    small = np.arange(blocks + 1)
    phi = 2 * np.pi * small[:, None] * (lane[None, :] + 0.5) / length
    twist = np.concatenate([np.cos(phi), np.sin(phi)], 1)
    index = small[:, None] + ring * shift[None, :]
    weight = np.where((small == 0) | (small == blocks), 1.0, 2.0)[:, None] / length
    weight = weight * (np.abs(index) <= kept) * valid
    slope = weight * 2 * np.pi * index / length
    factor = np.concatenate([weight, weight, slope, -slope], 1)
    latitude = (np.arange(lat_count) + 0.5) * (np.pi / lat_count) - 0.5 * np.pi
    secant = 1.0 / np.maximum(np.cos(latitude), cos_floor)
    line = np.zeros((8, lat_count))
    line[0] = secant / 60.0
    line[1] = coriolis * np.sin(latitude)
    parts = 2 * 3
    own = np.zeros((parts * ROWS, parts * ROWS))
    outer = np.zeros((parts * ROWS, parts * ROWS))
    for part in range(parts):
        for row in range(ROWS):
            for offset, value in ((1, 45.0), (2, -9.0), (3, 1.0)):
                for sign in (1, -1):
                    at = row + sign * offset
                    target = own if 0 <= at < ROWS else outer
                    target[part * ROWS + row, part * ROWS + at % ROWS] = sign * value
    own = np.concatenate([own, own], 1)
    outer = np.concatenate([outer, outer], 1)
    return (
        *np_split(forward),
        *np_split(inverse),
        jnp.asarray(twist.astype(np.float32)),
        jnp.asarray(factor.astype(np.float32)),
        jnp.asarray(line.astype(np.float32)),
        jnp.asarray(own.astype(np.float32)).astype(bf16),
        jnp.asarray(outer.astype(np.float32)).astype(bf16),
    )


def kernel(sizes, const_shapes, thick_ref, wind_ref, *refs):
    count = len(const_shapes)
    const_hbm, (out_h, out_w), scratch = refs[:count], refs[count : count + 2], refs[count + 2 :]
    const_refs, scratch = scratch[:count], scratch[count:]
    fwd_hi, fwd_lo, inv_hi, inv_lo, twist_ref, factor_ref, line_ref, own_ref, outer_ref = const_refs
    (
        state, halo, far, levels, spec_in, turned, zonal, smooth, slope, redo, const_sem, first_send, first_recv,
        far_send, far_recv, halo_send, halo_recv, lev_send, lev_recv, last_send, last_recv,
    ) = scratch
    lon_size, lev_size = sizes
    fields, _, lat_count = state.shape[1:]
    blocks = lat_count // LANES
    half = lon_size // 2
    chips = half // 2
    depth = 2 * lev_size
    lon, lev = lax.axis_index("lon"), lax.axis_index("lev")
    side_now = lon // half
    chip = (lon % half) // 2
    core = lon % 2
    odd = chip % 2
    z = side_now * lev_size + lev

    there = (z + lev_size // 2 + lev_size * ((odd + core + side_now) % 2)) % depth

    def owner(q):
        return {"lon": (there // lev_size) * half + 2 * chip + q, "lev": there % lev_size}

    place = (z + depth - lev_size // 2) % depth
    level = place % lev_size
    held_by = (place // lev_size + odd) % 2

    def holder(hemi):
        return {"lon": hemi * half + 2 * chip + held_by, "lev": level}

    across = (1 - side_now) * half + 2 * chip
    after = side_now * half + 2 * ((chip + 1) % chips)
    before = side_now * half + 2 * ((chip + chips - 1) % chips) + 1
    right = (1 - core) * (lon + 1) + core * ((1 - held_by) * across + held_by * after)
    left = core * (lon - 1) + (1 - core) * (held_by * (across + 1) + (1 - held_by) * before)
    swap_right = core * held_by * (chip // (chips - 1))
    swap_left = (1 - core) * (1 - held_by) * ((chips - 1 - chip) // (chips - 1))
    has_below, has_above = level > 0, level < lev_size - 1
    far_right, far_left = core * (1 - held_by), (1 - core) * held_by
    crossing = far_right + far_left
    beyond = (there + lev_size) % depth
    far_owner = {"lon": (beyond // lev_size) * half + 2 * chip + core, "lev": beyond % lev_size}

    def far_holder(hemi):
        return {"lon": hemi * half + 2 * chip + 1 - held_by, "lev": level}

    def at_height(height):
        return {"lon": (height // lev_size) * half + 2 * chip + core, "lev": height % lev_size}

    upward, downward = at_height((z + 1) % depth), at_height((z + depth - 1) % depth)

    loads = [pltpu.make_async_copy(const_hbm[n], const_refs[n], const_sem.at[n]) for n in range(count)]
    for copy in loads:
        copy.start()
    halo[...] = jnp.zeros_like(halo)
    far[...] = jnp.zeros_like(far)

    @pl.when(jnp.logical_not(has_below))
    def _():
        for s in range(STEPS):
            levels[s, 0] = jnp.zeros_like(levels[s, 0])

    @pl.when(jnp.logical_not(has_above))
    def _():
        for s in range(STEPS):
            levels[s, 1] = jnp.zeros_like(levels[s, 1])

    barrier = pltpu.get_barrier_semaphore()
    for device in (owner(0), owner(1), holder(0), holder(1), far_owner):
        pl.semaphore_signal(barrier, inc=1, device_id=device, device_id_type=MESH)

    for at, flag in ((left, far_left), (right, far_right)):

        @pl.when(flag == 0)
        def _(at=at):
            pl.semaphore_signal(barrier, inc=1, device_id={"lon": at}, device_id_type=MESH)

    @pl.when(crossing > 0)
    def _():
        for hemi in range(2):
            pl.semaphore_signal(barrier, inc=1, device_id=far_holder(hemi), device_id_type=MESH)

    @pl.when(has_below)
    def _():
        pl.semaphore_signal(barrier, inc=1, device_id=downward, device_id_type=MESH)

    @pl.when(has_above)
    def _():
        pl.semaphore_signal(barrier, inc=1, device_id=upward, device_id_type=MESH)

    def rows(part):
        return pl.ds(pl.multiple_of(part * ROWS, ROWS), ROWS)

    def first_copy(q, f, hemi):
        at = rows(q)
        return pltpu.make_async_remote_copy(
            src_ref=thick_ref.at[0, at] if f == 0 else wind_ref.at[f - 1, 0, at], dst_ref=state.at[0, f, rows(hemi)],
            send_sem=first_send.at[q, f], recv_sem=first_recv.at[hemi, f],
            device_id=owner(q), device_id_type=MESH,
        )

    def early_far_copy(f, side, hemi):
        at = pl.ds(2 * ROWS - 3 if side == 0 else 0, 3)
        return pltpu.make_async_remote_copy(
            src_ref=thick_ref.at[0, at] if f == 0 else wind_ref.at[f - 1, 0, at],
            dst_ref=far.at[0, f, hemi, pl.ds(ROWS - 3 if side == 0 else 0, 3)],
            send_sem=far_send.at[0, f, 0], recv_sem=far_recv.at[0, f, hemi],
            device_id=far_owner, device_id_type=MESH,
        )

    def last_copy(part, f, hemi, q, origin, span):
        start, length = span
        source = origin.at[f, pl.ds(hemi * ROWS + start, length)]
        at = pl.ds(q * ROWS + start, length)
        return pltpu.make_async_remote_copy(
            src_ref=source, dst_ref=out_h.at[0, at] if f == 0 else out_w.at[f - 1, 0, at],
            send_sem=last_send.at[part, hemi, f], recv_sem=last_recv.at[part, q, f],
            device_id=holder(hemi), device_id_type=MESH,
        )

    def halo_copy(s, side, f, hemi, distant=False):
        start = ROWS - 3 if side == 0 else 0
        to = hemi if distant else (hemi + (swap_right if side == 0 else swap_left)) % 2
        send, recv = far_send.at[s, f, hemi], far_recv.at[s, f, hemi]
        if not distant:
            send, recv = halo_send.at[s, side, f, hemi], halo_recv.at[s, side, f, to]
        return pltpu.make_async_remote_copy(
            src_ref=state.at[s, f, pl.ds(hemi * ROWS + start, 3)],
            dst_ref=(far if distant else halo).at[s, f, to, pl.ds(start, 3)],
            send_sem=send, recv_sem=recv,
            device_id={"lon": right if side == 0 else left}, device_id_type=MESH,
        )

    def lev_copy(s, side, hemi):
        return pltpu.make_async_remote_copy(
            src_ref=state.at[s, 0, rows(hemi)], dst_ref=levels.at[s, side, rows(hemi)],
            send_sem=lev_send.at[s, side, hemi], recv_sem=lev_recv.at[s, side, hemi],
            device_id=upward if side == 0 else downward, device_id_type=MESH,
        )

    whole, spans = (0, ROWS), {0: ((0, ROWS - 3), (ROWS - 3, 3)), 1: ((3, ROWS - 3), (0, 3))}

    def if_far(action):
        for side, flag in ((0, far_right), (1, far_left)):

            @pl.when(flag > 0)
            def _(side=side):
                action(side)

    def send_far(s):
        @if_far
        def _(side):
            for hemi in range(2):
                for f in range(fields):
                    halo_copy(s, side, f, hemi, True).start()

    def send_halo(s, hemi, chosen):
        for side, flag in ((0, far_right), (1, far_left)):

            @pl.when(flag == 0)
            def _(side=side):
                for f in chosen:
                    halo_copy(s, side, f, hemi).start()

    def near_halo(s, wait):
        for side, flag in ((0, far_left), (1, far_right)) if wait == "wait_recv" else ((0, far_right), (1, far_left)):

            @pl.when(flag == 0)
            def _(side=side):
                for f in range(fields):
                    for hemi in range(2):
                        getattr(halo_copy(s, side, f, hemi), wait)()

    def far_wait(s):
        for f in range(fields):
            for hemi in range(2):
                halo_copy(s, 1, f, hemi, True).wait_recv()

    def each_level(s, hemi, action):
        for side, flags in ((0, (has_above, has_below)), (1, (has_below, has_above))):

            @pl.when(flags[1 if action == "wait_recv" else 0])
            def _(side=side):
                getattr(lev_copy(s, side, hemi), action)()

    def product(value, high, low):
        top, rest = split(value)
        out = jnp.dot(top, low[...], preferred_element_type=f32)
        out += jnp.dot(rest, high[...], preferred_element_type=f32)
        return out + jnp.dot(top, high[...], preferred_element_type=f32)

    spectral = (blocks + 1) * 2 * ROWS

    def spectra(s, f):
        for hemi in range(2):
            r = slice(hemi * ROWS, (hemi + 1) * ROWS)
            values = [state[s, f, r, n * LANES : (n + 1) * LANES] for n in range(blocks)]
            for k, (re, im) in padded_transform(values).items():
                at = (2 * k + hemi) * ROWS
                c, d = twist_ref[k : k + 1, :LANES], twist_ref[k : k + 1, LANES:]
                if k == 0:
                    out = (re, jnp.zeros_like(re))
                elif im is None:
                    out = (re * c, -re * d)
                else:
                    out = (re * c + im * d, im * c - re * d)
                spec_in[at : at + ROWS, :LANES] = out[0]
                spec_in[at : at + ROWS, LANES:] = out[1]
        gains = product(spec_in[...], fwd_hi, fwd_lo)
        sign = 1.0 if f == 0 else -1.0
        for k in range(blocks + 1):
            at = 2 * k * ROWS
            to = at + ROWS
            end = to + ROWS
            a = gains[at:to, :LANES] + sign * gains[to:end, :LANES]
            b = gains[at:to, LANES:] - sign * gains[to:end, LANES:]
            w = factor_ref[k : k + 1]
            pieces = (a * w[:, :LANES], b * w[:, LANES : 2 * LANES])
            turned[at:to, :LANES] = pieces[0]
            turned[at:to, LANES:] = pieces[1]
            turned[to:end, :LANES] = sign * pieces[0]
            turned[to:end, LANES:] = -sign * pieces[1]
            at, to, end = at + spectral, to + spectral, end + spectral
            pieces = (b * w[:, 2 * LANES : 3 * LANES], a * w[:, 3 * LANES :])
            turned[at:to, :LANES] = pieces[0]
            turned[at:to, LANES:] = pieces[1]
            turned[to:end, :LANES] = -sign * pieces[0]
            turned[to:end, LANES:] = sign * pieces[1]
        turned[...] = product(turned[...], inv_hi, inv_lo)
        for which, target in enumerate((smooth, slope)):
            for hemi in range(2):
                terms = {}
                for k in range(blocks + 1):
                    at = which * spectral + (2 * k + hemi) * ROWS
                    re, im = turned[at : at + ROWS, :LANES], turned[at : at + ROWS, LANES:]
                    c, d = twist_ref[k : k + 1, :LANES], twist_ref[k : k + 1, LANES:]
                    if k == 0:
                        terms[k] = (re, None)
                    elif k == blocks:
                        terms[k] = (re * c - im * d, None)
                    else:
                        terms[k] = (re * c - im * d, re * d + im * c)
                r = slice(hemi * ROWS, (hemi + 1) * ROWS)
                for n, value in enumerate(padded_inverse(terms, blocks)):
                    target[f, r, n * LANES : (n + 1) * LANES] = value

    def own_zonal(s):
        value = state[s].reshape(fields * 2 * ROWS, lat_count)
        zonal[...] = jnp.dot(own_ref[...], jnp.concatenate(split(value), 0), preferred_element_type=f32)

    def outer_zonal(value):
        value = value.reshape(fields * 2 * ROWS, lat_count)
        zonal[...] += jnp.dot(outer_ref[...], jnp.concatenate(split(value), 0), preferred_element_type=f32)

    def advance(s, hemi, target):
        r = slice(hemi * ROWS, (hemi + 1) * ROWS)
        for n in range(blocks):
            lanes = slice(n * LANES, (n + 1) * LANES)
            h, u, v = (state[s, f, r, lanes] for f in range(fields))
            secant, turn = line_ref[0:1, lanes], line_ref[1:2, lanes]
            zh, zu, zv = (
                zonal[(2 * f + hemi) * ROWS : (2 * f + hemi + 1) * ROWS, lanes] * secant for f in range(fields)
            )
            mh, mu, mv = (slope[f, r, lanes] for f in range(fields))
            vertical = levels[s, 0, r, lanes] + levels[s, 1, r, lanes] - 2.0 * h
            th = mixing * vertical - (u * zh + v * mh) - h * (zu + mv)
            tu = turn * v - (u * zu + v * mu) - zh
            tv = -(u * zv + v * mv) - mh - turn * u
            for f, t in enumerate((th, tu, tv)):
                target[f, r, lanes] = smooth[f, r, lanes] + courant * t

    count_here = 7 + crossing + has_below.astype(jnp.int32) + has_above.astype(jnp.int32)
    pl.semaphore_wait(barrier, count_here)
    for f in range(fields):
        for q in range(2):
            first_copy(q, f, side_now).start()
        for side in range(2):

            @pl.when(core == side)
            def _(side=side):
                early_far_copy(f, side, side_now).start()

    for copy in loads:
        copy.wait()
    for s in range(STEPS):
        for f in range(fields):
            if s == 0:
                for hemi in range(2):
                    first_copy(core, f, hemi).wait_recv()
                    if f == 0:
                        each_level(0, hemi, "start")
                    send_halo(0, hemi, (f,))
            spectra(s, f)
        own_zonal(s)
        near_halo(s, "wait_recv")
        if s < STEPS - 1:

            @pl.when(crossing > 0)
            def _():
                far_wait(s)

            outer_zonal(halo[s] + far[s])
        else:
            outer_zonal(halo[s])
        for hemi in range(2):
            each_level(s, hemi, "wait_recv")
            target = state.at[s + 1]
            advance(s, hemi, target)
            if s < STEPS - 1:
                send_halo(s + 1, hemi, range(fields))
                each_level(s + 1, hemi, "start")
                if hemi == 1:
                    send_far(s + 1)
                continue

            @pl.when(crossing == 0)
            def _(hemi=hemi):
                for f in range(fields):
                    last_copy(0, f, hemi, core, target, whole).start()

            @if_far
            def _(side, hemi=hemi):
                for f in range(fields):
                    last_copy(0, f, hemi, 1 - side, target, spans[side][0]).start()

    @pl.when(crossing > 0)
    def _():
        far_wait(STEPS - 1)
        outer_zonal(far[STEPS - 1])
        for hemi in range(2):
            advance(STEPS - 1, hemi, redo)

            @if_far
            def _(side, hemi=hemi):
                for f in range(fields):
                    last_copy(1, f, hemi, 1 - side, redo, spans[side][1]).start()

    target = state.at[STEPS]
    for side in range(2):

        @pl.when(core == side)
        def _(side=side):
            for f in range(fields):
                last_copy(0, f, 0, side, target, whole).wait_recv()
                last_copy(0, f, 0, 1 - side, target, spans[side][0]).wait_recv()
                last_copy(1, f, 0, 1 - side, redo, spans[side][1]).wait_recv()

    for f in range(fields):
        for q in range(2):
            first_copy(q, f, side_now).wait_send()
        early_far_copy(f, 0, side_now).wait_send()
    for hemi in range(2):

        @pl.when(crossing == 0)
        def _(hemi=hemi):
            for f in range(fields):
                last_copy(0, f, hemi, core, target, whole).wait_send()

        @if_far
        def _(side, hemi=hemi):
            for f in range(fields):
                for s in range(1, STEPS):
                    halo_copy(s, side, f, hemi, True).wait_send()
                last_copy(0, f, hemi, 1 - side, target, spans[side][0]).wait_send()
                last_copy(1, f, hemi, 1 - side, redo, spans[side][1]).wait_send()

        for s in range(STEPS):
            each_level(s, hemi, "wait_send")
    for s in range(STEPS):
        near_halo(s, "wait_send")


def body(sizes, thickness, wind_field):
    level_count, lon_count, lat_count = thickness.shape
    fields = 3
    blocks = lat_count // LANES
    spectral = (blocks + 1) * 2 * ROWS
    consts = tables(lat_count)
    hbm = pl.BlockSpec(memory_space=pltpu.HBM)
    vmem = pl.BlockSpec(memory_space=pltpu.VMEM)
    dma = pltpu.SemaphoreType.DMA
    return pl.pallas_call(
        functools.partial(kernel, sizes, [c.shape for c in consts]),
        out_shape=(
            pltpu.VMEM(thickness.shape, f32),
            pltpu.VMEM(wind_field.shape, f32),
        ),
        in_specs=[hbm, hbm] + [hbm] * len(consts),
        out_specs=(vmem, vmem),
        scratch_shapes=[pltpu.VMEM(c.shape, c.dtype) for c in consts]
        + [
            pltpu.VMEM((STEPS + 1, fields, lon_count, lat_count), f32),
            pltpu.VMEM((STEPS, fields, 2, ROWS, lat_count), f32),
            pltpu.VMEM((STEPS, fields, 2, ROWS, lat_count), f32),
            pltpu.VMEM((STEPS, 2, lon_count, lat_count), f32),
            pltpu.VMEM((spectral, 2 * LANES), f32),
            pltpu.VMEM((2 * spectral, 2 * LANES), f32),
            pltpu.VMEM((fields * lon_count, lat_count), f32),
            pltpu.VMEM((fields, lon_count, lat_count), f32),
            pltpu.VMEM((fields, lon_count, lat_count), f32),
            pltpu.VMEM((fields, lon_count, lat_count), f32),
            dma((len(consts),)),
            dma((2, fields)),
            dma((2, fields)),
            dma((STEPS, fields, 2)),
            dma((STEPS, fields, 2)),
            dma((STEPS, 2, fields, 2)),
            dma((STEPS, 2, fields, 2)),
            dma((STEPS, 2, 2)),
            dma((STEPS, 2, 2)),
            dma((2, 2, fields)),
            dma((2, 2, fields)),
        ],
        name="sphere_steps",
        compiler_params=pltpu.CompilerParams(collective_id=0, has_side_effects=True, vmem_limit_bytes=66_200_000),
    )(thickness, wind_field, *consts)


def solution(mesh):
    sizes = (mesh.shape["lon"], mesh.shape["lev"])
    in_specs = (P("lev", "lon", None), P(None, "lev", "lon", None))
    out_specs = (P("lev", "lon", None), P(None, "lev", "lon", None))
    return jax.shard_map(
        functools.partial(body, sizes), mesh=mesh, in_specs=in_specs, out_specs=out_specs, check_vma=False
    )
```

```python
import functools
import math

import jax
import jax.numpy as jnp
import numpy as np
from jax import lax
from jax.experimental import pallas as pl
from jax.experimental.pallas import tpu as pltpu
from jax.sharding import PartitionSpec as P

STEPS = 2
MESH = pl.DeviceIdType.MESH

courant = 0.2
mixing = 0.25
coriolis = 0.5
cos_floor = 0.25

LANES = 128
ROWS = 8
f32 = jnp.float32
bf16 = jnp.bfloat16


def rotate(z, angle):
    re, im = z
    c, s = math.cos(angle), math.sin(angle)
    if abs(s) < 1e-12:
        return (re, im) if c > 0 else (-re, -im)
    if abs(c) < 1e-12:
        return (-im, re) if s > 0 else (im, -re)
    return re * c - im * s, re * s + im * c


def complex_sum(values, sign):
    count = len(values)
    if count == 1:
        return values
    half = count // 2
    plus = [(a[0] + b[0], a[1] + b[1]) for a, b in zip(values[:half], values[half:])]
    minus = [(a[0] - b[0], a[1] - b[1]) for a, b in zip(values[:half], values[half:])]
    minus = [rotate(z, sign * 2 * math.pi * n / count) for n, z in enumerate(minus)]
    even, odd = complex_sum(plus, sign), complex_sum(minus, sign)
    return [z for pair in zip(even, odd) for z in pair]


def odd_frequencies(values):
    count = len(values)
    if count == 1:
        return {1: (values[0], None)}
    half = count // 2
    joined = [rotate((values[n], -values[n + half]), -math.pi * n / count) for n in range(half)]
    out = {}
    for t, (re, im) in enumerate(complex_sum(joined, -1)):
        k = 4 * t + 1
        if k <= count:
            out[k] = (re, im)
        else:
            out[2 * count - k] = (re, -im)
    return out


def real_transform(values):
    count = len(values)
    if count == 1:
        return {0: (values[0], None)}
    half = count // 2
    even = real_transform([values[n] + values[n + half] for n in range(half)])
    out = {2 * k: z for k, z in even.items()}
    out.update(odd_frequencies([values[n] - values[n + half] for n in range(half)]))
    return out


def padded_transform(values):
    out = {2 * k: z for k, z in real_transform(values).items()}
    out.update(odd_frequencies(values))
    return out


def odd_inverse(terms, count):
    if count == 1:
        return [terms[1][0]]
    half = count // 2
    joined = []
    for t in range(half):
        k = 4 * t + 1
        if k <= count:
            joined.append(terms[k])
        else:
            re, im = terms[2 * count - k]
            joined.append((re, -im))
    turned = [rotate(z, math.pi * n / count) for n, z in enumerate(complex_sum(joined, 1))]
    return [z[0] for z in turned] + [-z[1] for z in turned]


def real_inverse(terms, count):
    if count == 1:
        return [terms[0][0]]
    half = count // 2
    even = real_inverse({k // 2: z for k, z in terms.items() if k % 2 == 0}, half)
    odd = odd_inverse({k: z for k, z in terms.items() if k % 2}, half)
    return [a + b for a, b in zip(even, odd)] + [a - b for a, b in zip(even, odd)]


def padded_inverse(terms, count):
    even = real_inverse({k // 2: z for k, z in terms.items() if k % 2 == 0}, count)
    odd = odd_inverse({k: z for k, z in terms.items() if k % 2}, count)
    return [a + b for a, b in zip(even, odd)]


def split(value):
    high = value.astype(bf16)
    return high, (value - high.astype(f32)).astype(bf16)


def np_split(table):
    table = jnp.asarray(table.astype(np.float32))
    high = table.astype(bf16)
    return high, (table - high.astype(f32)).astype(bf16)


def tables(lat_count):
    length = 2 * lat_count
    blocks = lat_count // LANES
    ring = 2 * blocks
    kept = length // 3
    reach = kept // ring + 1
    lane = np.arange(LANES)
    shift = np.where(lane < 2 * reach, lane - reach, 0)
    valid = (lane < 2 * reach).astype(np.float64)
    psi = 2 * np.pi * (lane[:, None] + 0.5) * shift[None, :] / LANES
    cos, sin = np.cos(psi) * valid, np.sin(psi) * valid
    forward = np.block([[cos, sin], [sin, -cos]])
    inverse = np.block([[cos.T, sin.T], [sin.T, -cos.T]])
    small = np.arange(blocks + 1)
    phi = 2 * np.pi * small[:, None] * (lane[None, :] + 0.5) / length
    twist = np.concatenate([np.cos(phi), np.sin(phi)], 1)
    index = small[:, None] + ring * shift[None, :]
    weight = np.where((small == 0) | (small == blocks), 1.0, 2.0)[:, None] / length
    weight = weight * (np.abs(index) <= kept) * valid
    slope = weight * 2 * np.pi * index / length
    factor = np.concatenate([weight, weight, slope, -slope], 1)
    latitude = (np.arange(lat_count) + 0.5) * (np.pi / lat_count) - 0.5 * np.pi
    secant = 1.0 / np.maximum(np.cos(latitude), cos_floor)
    line = np.zeros((8, lat_count))
    line[0] = secant / 60.0
    line[1] = coriolis * np.sin(latitude)
    parts = 2 * 3
    own = np.zeros((parts * ROWS, parts * ROWS))
    outer = np.zeros((parts * ROWS, parts * ROWS))
    for part in range(parts):
        for row in range(ROWS):
            for offset, value in ((1, 45.0), (2, -9.0), (3, 1.0)):
                for sign in (1, -1):
                    at = row + sign * offset
                    target = own if 0 <= at < ROWS else outer
                    target[part * ROWS + row, part * ROWS + at % ROWS] = sign * value
    own = np.concatenate([own, own], 1)
    outer = np.concatenate([outer, outer], 1)
    return (
        *np_split(forward),
        *np_split(inverse),
        jnp.asarray(twist.astype(np.float32)),
        jnp.asarray(factor.astype(np.float32)),
        jnp.asarray(line.astype(np.float32)),
        jnp.asarray(own.astype(np.float32)).astype(bf16),
        jnp.asarray(outer.astype(np.float32)).astype(bf16),
    )


def kernel(sizes, const_shapes, thick_ref, wind_ref, *refs):
    count = len(const_shapes)
    const_hbm, (out_h, out_w), scratch = refs[:count], refs[count : count + 2], refs[count + 2 :]
    const_refs, scratch = scratch[:count], scratch[count:]
    fwd_hi, fwd_lo, inv_hi, inv_lo, twist_ref, factor_ref, line_ref, own_ref, outer_ref = const_refs
    (
        state, halo, far, levels, spec_in, turned, zonal, smooth, slope, redo, const_sem, first_send, first_recv,
        far_send, far_recv, halo_send, halo_recv, lev_send, lev_recv, last_send, last_recv,
    ) = scratch
    lon_size, lev_size = sizes
    fields, _, lat_count = state.shape[1:]
    blocks = lat_count // LANES
    half = lon_size // 2
    chips = half // 2
    depth = 2 * lev_size
    lon, lev = lax.axis_index("lon"), lax.axis_index("lev")
    side_now = lon // half
    chip = (lon % half) // 2
    core = lon % 2
    odd = chip % 2
    z = side_now * lev_size + lev

    there = (z + lev_size // 2 + lev_size * ((odd + core + side_now) % 2)) % depth

    def owner(q):
        return {"lon": (there // lev_size) * half + 2 * chip + q, "lev": there % lev_size}

    place = (z + depth - lev_size // 2) % depth
    level = place % lev_size
    held_by = (place // lev_size + odd) % 2

    def holder(hemi):
        return {"lon": hemi * half + 2 * chip + held_by, "lev": level}

    across = (1 - side_now) * half + 2 * chip
    after = side_now * half + 2 * ((chip + 1) % chips)
    before = side_now * half + 2 * ((chip + chips - 1) % chips) + 1
    right = (1 - core) * (lon + 1) + core * ((1 - held_by) * across + held_by * after)
    left = core * (lon - 1) + (1 - core) * (held_by * (across + 1) + (1 - held_by) * before)
    swap_right = core * held_by * (chip // (chips - 1))
    swap_left = (1 - core) * (1 - held_by) * ((chips - 1 - chip) // (chips - 1))
    has_below, has_above = level > 0, level < lev_size - 1
    far_right, far_left = core * (1 - held_by), (1 - core) * held_by
    crossing = far_right + far_left
    beyond = (there + lev_size) % depth
    far_owner = {"lon": (beyond // lev_size) * half + 2 * chip + core, "lev": beyond % lev_size}

    def far_holder(hemi):
        return {"lon": hemi * half + 2 * chip + 1 - held_by, "lev": level}

    def at_height(height):
        return {"lon": (height // lev_size) * half + 2 * chip + core, "lev": height % lev_size}

    upward, downward = at_height((z + 1) % depth), at_height((z + depth - 1) % depth)

    loads = [pltpu.make_async_copy(const_hbm[n], const_refs[n], const_sem.at[n]) for n in range(count)]
    for copy in loads:
        copy.start()
    halo[...] = jnp.zeros_like(halo)
    far[...] = jnp.zeros_like(far)

    @pl.when(jnp.logical_not(has_below))
    def _():
        for s in range(STEPS):
            levels[s, 0] = jnp.zeros_like(levels[s, 0])

    @pl.when(jnp.logical_not(has_above))
    def _():
        for s in range(STEPS):
            levels[s, 1] = jnp.zeros_like(levels[s, 1])

    barrier = pltpu.get_barrier_semaphore()
    for device in (owner(0), owner(1), holder(0), holder(1), far_owner):
        pl.semaphore_signal(barrier, inc=1, device_id=device, device_id_type=MESH)

    for at, flag in ((left, far_left), (right, far_right)):

        @pl.when(flag == 0)
        def _(at=at):
            pl.semaphore_signal(barrier, inc=1, device_id={"lon": at}, device_id_type=MESH)

    @pl.when(crossing > 0)
    def _():
        for hemi in range(2):
            pl.semaphore_signal(barrier, inc=1, device_id=far_holder(hemi), device_id_type=MESH)

    @pl.when(has_below)
    def _():
        pl.semaphore_signal(barrier, inc=1, device_id=downward, device_id_type=MESH)

    @pl.when(has_above)
    def _():
        pl.semaphore_signal(barrier, inc=1, device_id=upward, device_id_type=MESH)

    def rows(part):
        return pl.ds(pl.multiple_of(part * ROWS, ROWS), ROWS)

    def first_copy(q, f, hemi):
        at = rows(q)
        return pltpu.make_async_remote_copy(
            src_ref=thick_ref.at[0, at] if f == 0 else wind_ref.at[f - 1, 0, at], dst_ref=state.at[0, f, rows(hemi)],
            send_sem=first_send.at[q, f], recv_sem=first_recv.at[hemi, f],
            device_id=owner(q), device_id_type=MESH,
        )

    def early_far_copy(f, side, hemi):
        at = pl.ds(2 * ROWS - 3 if side == 0 else 0, 3)
        return pltpu.make_async_remote_copy(
            src_ref=thick_ref.at[0, at] if f == 0 else wind_ref.at[f - 1, 0, at],
            dst_ref=far.at[0, f, hemi, pl.ds(ROWS - 3 if side == 0 else 0, 3)],
            send_sem=far_send.at[0, f, 0], recv_sem=far_recv.at[0, f, hemi],
            device_id=far_owner, device_id_type=MESH,
        )

    def last_copy(part, f, hemi, q, origin, span):
        start, length = span
        source = origin.at[f, pl.ds(hemi * ROWS + start, length)]
        at = pl.ds(q * ROWS + start, length)
        return pltpu.make_async_remote_copy(
            src_ref=source, dst_ref=out_h.at[0, at] if f == 0 else out_w.at[f - 1, 0, at],
            send_sem=last_send.at[part, hemi, f], recv_sem=last_recv.at[part, q, f],
            device_id=holder(hemi), device_id_type=MESH,
        )

    def halo_copy(s, side, f, hemi, distant=False):
        start = ROWS - 3 if side == 0 else 0
        to = hemi if distant else (hemi + (swap_right if side == 0 else swap_left)) % 2
        send, recv = far_send.at[s, f, hemi], far_recv.at[s, f, hemi]
        if not distant:
            send, recv = halo_send.at[s, side, f, hemi], halo_recv.at[s, side, f, to]
        return pltpu.make_async_remote_copy(
            src_ref=state.at[s, f, pl.ds(hemi * ROWS + start, 3)],
            dst_ref=(far if distant else halo).at[s, f, to, pl.ds(start, 3)],
            send_sem=send, recv_sem=recv,
            device_id={"lon": right if side == 0 else left}, device_id_type=MESH,
        )

    def lev_copy(s, side, hemi):
        return pltpu.make_async_remote_copy(
            src_ref=state.at[s, 0, rows(hemi)], dst_ref=levels.at[s, side, rows(hemi)],
            send_sem=lev_send.at[s, side, hemi], recv_sem=lev_recv.at[s, side, hemi],
            device_id=upward if side == 0 else downward, device_id_type=MESH,
        )

    whole, spans = (0, ROWS), {0: ((0, ROWS - 3), (ROWS - 3, 3)), 1: ((3, ROWS - 3), (0, 3))}

    def if_far(action):
        for side, flag in ((0, far_right), (1, far_left)):

            @pl.when(flag > 0)
            def _(side=side):
                action(side)

    def send_far(s, hemi):
        @if_far
        def _(side):
            for f in range(fields):
                halo_copy(s, side, f, hemi, True).start()

    def send_halo(s, hemi, chosen):
        for side, flag in ((0, far_right), (1, far_left)):

            @pl.when(flag == 0)
            def _(side=side):
                for f in chosen:
                    halo_copy(s, side, f, hemi).start()

    def near_halo(s, wait):
        for side, flag in ((0, far_left), (1, far_right)) if wait == "wait_recv" else ((0, far_right), (1, far_left)):

            @pl.when(flag == 0)
            def _(side=side):
                for f in range(fields):
                    for hemi in range(2):
                        getattr(halo_copy(s, side, f, hemi), wait)()

    def far_wait(s):
        for f in range(fields):
            for hemi in range(2):
                halo_copy(s, 1, f, hemi, True).wait_recv()

    def each_level(s, hemi, action):
        for side, flags in ((0, (has_above, has_below)), (1, (has_below, has_above))):

            @pl.when(flags[1 if action == "wait_recv" else 0])
            def _(side=side):
                getattr(lev_copy(s, side, hemi), action)()

    def product(value, high, low):
        top, rest = split(value)
        out = jnp.dot(top, low[...], preferred_element_type=f32)
        out += jnp.dot(rest, high[...], preferred_element_type=f32)
        return out + jnp.dot(top, high[...], preferred_element_type=f32)

    spectral = (blocks + 1) * 2 * ROWS

    def spectra(s, f):
        for hemi in range(2):
            r = slice(hemi * ROWS, (hemi + 1) * ROWS)
            values = [state[s, f, r, n * LANES : (n + 1) * LANES] for n in range(blocks)]
            for k, (re, im) in padded_transform(values).items():
                at = (2 * k + hemi) * ROWS
                c, d = twist_ref[k : k + 1, :LANES], twist_ref[k : k + 1, LANES:]
                if k == 0:
                    out = (re, jnp.zeros_like(re))
                elif im is None:
                    out = (re * c, -re * d)
                else:
                    out = (re * c + im * d, im * c - re * d)
                spec_in[at : at + ROWS, :LANES] = out[0]
                spec_in[at : at + ROWS, LANES:] = out[1]
        gains = product(spec_in[...], fwd_hi, fwd_lo)
        sign = 1.0 if f == 0 else -1.0
        for k in range(blocks + 1):
            at = 2 * k * ROWS
            to = at + ROWS
            end = to + ROWS
            a = gains[at:to, :LANES] + sign * gains[to:end, :LANES]
            b = gains[at:to, LANES:] - sign * gains[to:end, LANES:]
            w = factor_ref[k : k + 1]
            pieces = (a * w[:, :LANES], b * w[:, LANES : 2 * LANES])
            turned[at:to, :LANES] = pieces[0]
            turned[at:to, LANES:] = pieces[1]
            turned[to:end, :LANES] = sign * pieces[0]
            turned[to:end, LANES:] = -sign * pieces[1]
            at, to, end = at + spectral, to + spectral, end + spectral
            pieces = (b * w[:, 2 * LANES : 3 * LANES], a * w[:, 3 * LANES :])
            turned[at:to, :LANES] = pieces[0]
            turned[at:to, LANES:] = pieces[1]
            turned[to:end, :LANES] = -sign * pieces[0]
            turned[to:end, LANES:] = sign * pieces[1]
        turned[...] = product(turned[...], inv_hi, inv_lo)
        for which, target in enumerate((smooth, slope)):
            for hemi in range(2):
                terms = {}
                for k in range(blocks + 1):
                    at = which * spectral + (2 * k + hemi) * ROWS
                    re, im = turned[at : at + ROWS, :LANES], turned[at : at + ROWS, LANES:]
                    c, d = twist_ref[k : k + 1, :LANES], twist_ref[k : k + 1, LANES:]
                    if k == 0:
                        terms[k] = (re, None)
                    elif k == blocks:
                        terms[k] = (re * c - im * d, None)
                    else:
                        terms[k] = (re * c - im * d, re * d + im * c)
                r = slice(hemi * ROWS, (hemi + 1) * ROWS)
                for n, value in enumerate(padded_inverse(terms, blocks)):
                    target[f, r, n * LANES : (n + 1) * LANES] = value

    def own_zonal(s):
        value = state[s].reshape(fields * 2 * ROWS, lat_count)
        zonal[...] = jnp.dot(own_ref[...], jnp.concatenate(split(value), 0), preferred_element_type=f32)

    def outer_zonal(value):
        value = value.reshape(fields * 2 * ROWS, lat_count)
        zonal[...] += jnp.dot(outer_ref[...], jnp.concatenate(split(value), 0), preferred_element_type=f32)

    def advance(s, hemi, target):
        r = slice(hemi * ROWS, (hemi + 1) * ROWS)
        for n in range(blocks):
            lanes = slice(n * LANES, (n + 1) * LANES)
            h, u, v = (state[s, f, r, lanes] for f in range(fields))
            secant, turn = line_ref[0:1, lanes], line_ref[1:2, lanes]
            zh, zu, zv = (
                zonal[(2 * f + hemi) * ROWS : (2 * f + hemi + 1) * ROWS, lanes] * secant for f in range(fields)
            )
            mh, mu, mv = (slope[f, r, lanes] for f in range(fields))
            vertical = levels[s, 0, r, lanes] + levels[s, 1, r, lanes] - 2.0 * h
            th = mixing * vertical - (u * zh + v * mh) - h * (zu + mv)
            tu = turn * v - (u * zu + v * mu) - zh
            tv = -(u * zv + v * mv) - mh - turn * u
            for f, t in enumerate((th, tu, tv)):
                target[f, r, lanes] = smooth[f, r, lanes] + courant * t

    count_here = 7 + crossing + has_below.astype(jnp.int32) + has_above.astype(jnp.int32)
    pl.semaphore_wait(barrier, count_here)
    for f in range(fields):
        for q in range(2):
            first_copy(q, f, side_now).start()
        for side in range(2):

            @pl.when(core == side)
            def _(side=side):
                early_far_copy(f, side, side_now).start()

    for copy in loads:
        copy.wait()
    for s in range(STEPS):
        for f in range(fields):
            if s == 0:
                for hemi in range(2):
                    first_copy(core, f, hemi).wait_recv()
                    if f == 0:
                        each_level(0, hemi, "start")
                    send_halo(0, hemi, (f,))
            spectra(s, f)
        own_zonal(s)
        near_halo(s, "wait_recv")
        if s < STEPS - 1:

            @pl.when(crossing > 0)
            def _():
                far_wait(s)

            outer_zonal(halo[s] + far[s])
        else:
            outer_zonal(halo[s])
        for hemi in range(2):
            each_level(s, hemi, "wait_recv")
            target = state.at[s + 1]
            advance(s, hemi, target)
            if s < STEPS - 1:
                send_far(s + 1, hemi)
                send_halo(s + 1, hemi, range(fields))
                each_level(s + 1, hemi, "start")
                continue

            @pl.when(crossing == 0)
            def _(hemi=hemi):
                for f in range(fields):
                    last_copy(0, f, hemi, core, target, whole).start()

            @if_far
            def _(side, hemi=hemi):
                for f in range(fields):
                    last_copy(0, f, hemi, 1 - side, target, spans[side][0]).start()

    @pl.when(crossing > 0)
    def _():
        far_wait(STEPS - 1)
        outer_zonal(far[STEPS - 1])
        for hemi in range(2):
            advance(STEPS - 1, hemi, redo)

            @if_far
            def _(side, hemi=hemi):
                for f in range(fields):
                    last_copy(1, f, hemi, 1 - side, redo, spans[side][1]).start()

    target = state.at[STEPS]
    for side in range(2):

        @pl.when(core == side)
        def _(side=side):
            for f in range(fields):
                last_copy(0, f, 0, side, target, whole).wait_recv()
                last_copy(0, f, 0, 1 - side, target, spans[side][0]).wait_recv()
                last_copy(1, f, 0, 1 - side, redo, spans[side][1]).wait_recv()

    for f in range(fields):
        for q in range(2):
            first_copy(q, f, side_now).wait_send()
        early_far_copy(f, 0, side_now).wait_send()
    for hemi in range(2):

        @pl.when(crossing == 0)
        def _(hemi=hemi):
            for f in range(fields):
                last_copy(0, f, hemi, core, target, whole).wait_send()

        @if_far
        def _(side, hemi=hemi):
            for f in range(fields):
                for s in range(1, STEPS):
                    halo_copy(s, side, f, hemi, True).wait_send()
                last_copy(0, f, hemi, 1 - side, target, spans[side][0]).wait_send()
                last_copy(1, f, hemi, 1 - side, redo, spans[side][1]).wait_send()

        for s in range(STEPS):
            each_level(s, hemi, "wait_send")
    for s in range(STEPS):
        near_halo(s, "wait_send")


def body(sizes, thickness, wind_field):
    level_count, lon_count, lat_count = thickness.shape
    fields = 3
    blocks = lat_count // LANES
    spectral = (blocks + 1) * 2 * ROWS
    consts = tables(lat_count)
    hbm = pl.BlockSpec(memory_space=pltpu.HBM)
    vmem = pl.BlockSpec(memory_space=pltpu.VMEM)
    dma = pltpu.SemaphoreType.DMA
    return pl.pallas_call(
        functools.partial(kernel, sizes, [c.shape for c in consts]),
        out_shape=(
            pltpu.VMEM(thickness.shape, f32),
            pltpu.VMEM(wind_field.shape, f32),
        ),
        in_specs=[hbm, hbm] + [hbm] * len(consts),
        out_specs=(vmem, vmem),
        scratch_shapes=[pltpu.VMEM(c.shape, c.dtype) for c in consts]
        + [
            pltpu.VMEM((STEPS + 1, fields, lon_count, lat_count), f32),
            pltpu.VMEM((STEPS, fields, 2, ROWS, lat_count), f32),
            pltpu.VMEM((STEPS, fields, 2, ROWS, lat_count), f32),
            pltpu.VMEM((STEPS, 2, lon_count, lat_count), f32),
            pltpu.VMEM((spectral, 2 * LANES), f32),
            pltpu.VMEM((2 * spectral, 2 * LANES), f32),
            pltpu.VMEM((fields * lon_count, lat_count), f32),
            pltpu.VMEM((fields, lon_count, lat_count), f32),
            pltpu.VMEM((fields, lon_count, lat_count), f32),
            pltpu.VMEM((fields, lon_count, lat_count), f32),
            dma((len(consts),)),
            dma((2, fields)),
            dma((2, fields)),
            dma((STEPS, fields, 2)),
            dma((STEPS, fields, 2)),
            dma((STEPS, 2, fields, 2)),
            dma((STEPS, 2, fields, 2)),
            dma((STEPS, 2, 2)),
            dma((STEPS, 2, 2)),
            dma((2, 2, fields)),
            dma((2, 2, fields)),
        ],
        name="sphere_steps",
        compiler_params=pltpu.CompilerParams(collective_id=0, has_side_effects=True, vmem_limit_bytes=66_200_000),
    )(thickness, wind_field, *consts)


def solution(mesh):
    sizes = (mesh.shape["lon"], mesh.shape["lev"])
    in_specs = (P("lev", "lon", None), P(None, "lev", "lon", None))
    out_specs = (P("lev", "lon", None), P(None, "lev", "lon", None))
    return jax.shard_map(
        functools.partial(body, sizes), mesh=mesh, in_specs=in_specs, out_specs=out_specs, check_vma=False
    )
```

```python
import functools
import math

import jax
import jax.numpy as jnp
import numpy as np
from jax import lax
from jax.experimental import pallas as pl
from jax.experimental.pallas import tpu as pltpu
from jax.sharding import PartitionSpec as P

STEPS = 2
MESH = pl.DeviceIdType.MESH

courant = 0.2
mixing = 0.25
coriolis = 0.5
cos_floor = 0.25

LANES = 128
ROWS = 8
f32 = jnp.float32
bf16 = jnp.bfloat16


def rotate(z, angle):
    re, im = z
    c, s = math.cos(angle), math.sin(angle)
    if abs(s) < 1e-12:
        return (re, im) if c > 0 else (-re, -im)
    if abs(c) < 1e-12:
        return (-im, re) if s > 0 else (im, -re)
    return re * c - im * s, re * s + im * c


def complex_sum(values, sign):
    count = len(values)
    if count == 1:
        return values
    half = count // 2
    plus = [(a[0] + b[0], a[1] + b[1]) for a, b in zip(values[:half], values[half:])]
    minus = [(a[0] - b[0], a[1] - b[1]) for a, b in zip(values[:half], values[half:])]
    minus = [rotate(z, sign * 2 * math.pi * n / count) for n, z in enumerate(minus)]
    even, odd = complex_sum(plus, sign), complex_sum(minus, sign)
    return [z for pair in zip(even, odd) for z in pair]


def odd_frequencies(values):
    count = len(values)
    if count == 1:
        return {1: (values[0], None)}
    half = count // 2
    joined = [rotate((values[n], -values[n + half]), -math.pi * n / count) for n in range(half)]
    out = {}
    for t, (re, im) in enumerate(complex_sum(joined, -1)):
        k = 4 * t + 1
        if k <= count:
            out[k] = (re, im)
        else:
            out[2 * count - k] = (re, -im)
    return out


def real_transform(values):
    count = len(values)
    if count == 1:
        return {0: (values[0], None)}
    half = count // 2
    even = real_transform([values[n] + values[n + half] for n in range(half)])
    out = {2 * k: z for k, z in even.items()}
    out.update(odd_frequencies([values[n] - values[n + half] for n in range(half)]))
    return out


def padded_transform(values):
    out = {2 * k: z for k, z in real_transform(values).items()}
    out.update(odd_frequencies(values))
    return out


def odd_inverse(terms, count):
    if count == 1:
        return [terms[1][0]]
    half = count // 2
    joined = []
    for t in range(half):
        k = 4 * t + 1
        if k <= count:
            joined.append(terms[k])
        else:
            re, im = terms[2 * count - k]
            joined.append((re, -im))
    turned = [rotate(z, math.pi * n / count) for n, z in enumerate(complex_sum(joined, 1))]
    return [z[0] for z in turned] + [-z[1] for z in turned]


def real_inverse(terms, count):
    if count == 1:
        return [terms[0][0]]
    half = count // 2
    even = real_inverse({k // 2: z for k, z in terms.items() if k % 2 == 0}, half)
    odd = odd_inverse({k: z for k, z in terms.items() if k % 2}, half)
    return [a + b for a, b in zip(even, odd)] + [a - b for a, b in zip(even, odd)]


def padded_inverse(terms, count):
    even = real_inverse({k // 2: z for k, z in terms.items() if k % 2 == 0}, count)
    odd = odd_inverse({k: z for k, z in terms.items() if k % 2}, count)
    return [a + b for a, b in zip(even, odd)]


def split(value):
    high = value.astype(bf16)
    return high, (value - high.astype(f32)).astype(bf16)


def np_split(table):
    table = jnp.asarray(table.astype(np.float32))
    high = table.astype(bf16)
    return high, (table - high.astype(f32)).astype(bf16)


def tables(lat_count):
    length = 2 * lat_count
    blocks = lat_count // LANES
    ring = 2 * blocks
    kept = length // 3
    reach = kept // ring + 1
    lane = np.arange(LANES)
    shift = np.where(lane < 2 * reach, lane - reach, 0)
    valid = (lane < 2 * reach).astype(np.float64)
    psi = 2 * np.pi * (lane[:, None] + 0.5) * shift[None, :] / LANES
    cos, sin = np.cos(psi) * valid, np.sin(psi) * valid
    forward = np.block([[cos, sin], [sin, -cos]])
    inverse = np.block([[cos.T, sin.T], [sin.T, -cos.T]])
    small = np.arange(blocks + 1)
    phi = 2 * np.pi * small[:, None] * (lane[None, :] + 0.5) / length
    twist = np.concatenate([np.cos(phi), np.sin(phi)], 1)
    index = small[:, None] + ring * shift[None, :]
    weight = np.where((small == 0) | (small == blocks), 1.0, 2.0)[:, None] / length
    weight = weight * (np.abs(index) <= kept) * valid
    slope = weight * 2 * np.pi * index / length
    factor = np.concatenate([weight, weight, slope, -slope], 1)
    latitude = (np.arange(lat_count) + 0.5) * (np.pi / lat_count) - 0.5 * np.pi
    secant = 1.0 / np.maximum(np.cos(latitude), cos_floor)
    line = np.zeros((8, lat_count))
    line[0] = secant / 60.0
    line[1] = coriolis * np.sin(latitude)
    parts = 2 * 3
    own = np.zeros((parts * ROWS, parts * ROWS))
    outer = np.zeros((parts * ROWS, parts * ROWS))
    for part in range(parts):
        for row in range(ROWS):
            for offset, value in ((1, 45.0), (2, -9.0), (3, 1.0)):
                for sign in (1, -1):
                    at = row + sign * offset
                    target = own if 0 <= at < ROWS else outer
                    target[part * ROWS + row, part * ROWS + at % ROWS] = sign * value
    own = np.concatenate([own, own], 1)
    outer = np.concatenate([outer, outer], 1)
    return (
        *np_split(forward),
        *np_split(inverse),
        jnp.asarray(twist.astype(np.float32)),
        jnp.asarray(factor.astype(np.float32)),
        jnp.asarray(line.astype(np.float32)),
        jnp.asarray(own.astype(np.float32)).astype(bf16),
        jnp.asarray(outer.astype(np.float32)).astype(bf16),
    )


def kernel(sizes, const_shapes, thick_ref, wind_ref, *refs):
    count = len(const_shapes)
    const_hbm, (out_h, out_w), scratch = refs[:count], refs[count : count + 2], refs[count + 2 :]
    const_refs, scratch = scratch[:count], scratch[count:]
    fwd_hi, fwd_lo, inv_hi, inv_lo, twist_ref, factor_ref, line_ref, own_ref, outer_ref = const_refs
    (
        state, halo, far, levels, spec_in, turned, zonal, smooth, slope, redo, const_sem, first_send, first_recv,
        far_send, far_recv, halo_send, halo_recv, lev_send, lev_recv, last_send, last_recv,
    ) = scratch
    lon_size, lev_size = sizes
    fields, _, lat_count = state.shape[1:]
    blocks = lat_count // LANES
    half = lon_size // 2
    chips = half // 2
    depth = 2 * lev_size
    lon, lev = lax.axis_index("lon"), lax.axis_index("lev")
    side_now = lon // half
    chip = (lon % half) // 2
    core = lon % 2
    odd = chip % 2
    z = side_now * lev_size + lev

    there = (z + lev_size // 2 + lev_size * ((odd + core + side_now) % 2)) % depth

    def owner(q):
        return {"lon": (there // lev_size) * half + 2 * chip + q, "lev": there % lev_size}

    place = (z + depth - lev_size // 2) % depth
    level = place % lev_size
    held_by = (place // lev_size + odd) % 2

    def holder(hemi):
        return {"lon": hemi * half + 2 * chip + held_by, "lev": level}

    across = (1 - side_now) * half + 2 * chip
    after = side_now * half + 2 * ((chip + 1) % chips)
    before = side_now * half + 2 * ((chip + chips - 1) % chips) + 1
    right = (1 - core) * (lon + 1) + core * ((1 - held_by) * across + held_by * after)
    left = core * (lon - 1) + (1 - core) * (held_by * (across + 1) + (1 - held_by) * before)
    swap_right = core * held_by * (chip // (chips - 1))
    swap_left = (1 - core) * (1 - held_by) * ((chips - 1 - chip) // (chips - 1))
    has_below, has_above = level > 0, level < lev_size - 1
    far_right, far_left = core * (1 - held_by), (1 - core) * held_by
    crossing = far_right + far_left
    beyond = (there + lev_size) % depth
    far_owner = {"lon": (beyond // lev_size) * half + 2 * chip + core, "lev": beyond % lev_size}

    def far_holder(hemi):
        return {"lon": hemi * half + 2 * chip + 1 - held_by, "lev": level}

    def at_height(height):
        return {"lon": (height // lev_size) * half + 2 * chip + core, "lev": height % lev_size}

    upward, downward = at_height((z + 1) % depth), at_height((z + depth - 1) % depth)

    loads = [pltpu.make_async_copy(const_hbm[n], const_refs[n], const_sem.at[n]) for n in range(count)]
    for copy in loads:
        copy.start()
    halo[...] = jnp.zeros_like(halo)
    far[...] = jnp.zeros_like(far)

    @pl.when(jnp.logical_not(has_below))
    def _():
        for s in range(STEPS):
            levels[s, 0] = jnp.zeros_like(levels[s, 0])

    @pl.when(jnp.logical_not(has_above))
    def _():
        for s in range(STEPS):
            levels[s, 1] = jnp.zeros_like(levels[s, 1])

    barrier = pltpu.get_barrier_semaphore()
    for device in (owner(0), owner(1), holder(0), holder(1), far_owner):
        pl.semaphore_signal(barrier, inc=1, device_id=device, device_id_type=MESH)

    for at, flag in ((left, far_left), (right, far_right)):

        @pl.when(flag == 0)
        def _(at=at):
            pl.semaphore_signal(barrier, inc=1, device_id={"lon": at}, device_id_type=MESH)

    @pl.when(crossing > 0)
    def _():
        for hemi in range(2):
            pl.semaphore_signal(barrier, inc=1, device_id=far_holder(hemi), device_id_type=MESH)

    @pl.when(has_below)
    def _():
        pl.semaphore_signal(barrier, inc=1, device_id=downward, device_id_type=MESH)

    @pl.when(has_above)
    def _():
        pl.semaphore_signal(barrier, inc=1, device_id=upward, device_id_type=MESH)

    def rows(part):
        return pl.ds(pl.multiple_of(part * ROWS, ROWS), ROWS)

    def first_copy(q, f, hemi):
        at = rows(q)
        return pltpu.make_async_remote_copy(
            src_ref=thick_ref.at[0, at] if f == 0 else wind_ref.at[f - 1, 0, at], dst_ref=state.at[0, f, rows(hemi)],
            send_sem=first_send.at[q, f], recv_sem=first_recv.at[hemi, f],
            device_id=owner(q), device_id_type=MESH,
        )

    def early_far_copy(f, side, hemi):
        at = pl.ds(2 * ROWS - 3 if side == 0 else 0, 3)
        return pltpu.make_async_remote_copy(
            src_ref=thick_ref.at[0, at] if f == 0 else wind_ref.at[f - 1, 0, at],
            dst_ref=far.at[0, f, hemi, pl.ds(ROWS - 3 if side == 0 else 0, 3)],
            send_sem=far_send.at[0, f, 0], recv_sem=far_recv.at[0, f, hemi],
            device_id=far_owner, device_id_type=MESH,
        )

    def last_copy(part, f, hemi, q, origin, span):
        start, length = span
        source = origin.at[f, pl.ds(hemi * ROWS + start, length)]
        at = pl.ds(q * ROWS + start, length)
        return pltpu.make_async_remote_copy(
            src_ref=source, dst_ref=out_h.at[0, at] if f == 0 else out_w.at[f - 1, 0, at],
            send_sem=last_send.at[part, hemi, f], recv_sem=last_recv.at[part, q, f],
            device_id=holder(hemi), device_id_type=MESH,
        )

    def halo_copy(s, side, f, hemi, distant=False):
        start = ROWS - 3 if side == 0 else 0
        to = hemi if distant else (hemi + (swap_right if side == 0 else swap_left)) % 2
        send, recv = far_send.at[s, f, hemi], far_recv.at[s, f, hemi]
        if not distant:
            send, recv = halo_send.at[s, side, f, hemi], halo_recv.at[s, side, f, to]
        return pltpu.make_async_remote_copy(
            src_ref=state.at[s, f, pl.ds(hemi * ROWS + start, 3)],
            dst_ref=(far if distant else halo).at[s, f, to, pl.ds(start, 3)],
            send_sem=send, recv_sem=recv,
            device_id={"lon": right if side == 0 else left}, device_id_type=MESH,
        )

    def lev_copy(s, side, hemi):
        return pltpu.make_async_remote_copy(
            src_ref=state.at[s, 0, rows(hemi)], dst_ref=levels.at[s, side, rows(hemi)],
            send_sem=lev_send.at[s, side, hemi], recv_sem=lev_recv.at[s, side, hemi],
            device_id=upward if side == 0 else downward, device_id_type=MESH,
        )

    whole, spans = (0, ROWS), {0: ((0, ROWS - 3), (ROWS - 3, 3)), 1: ((3, ROWS - 3), (0, 3))}

    def if_far(action):
        for side, flag in ((0, far_right), (1, far_left)):

            @pl.when(flag > 0)
            def _(side=side):
                action(side)

    def send_far(s, hemi):
        @if_far
        def _(side):
            for f in range(fields):
                halo_copy(s, side, f, hemi, True).start()

    def send_halo(s, hemi, chosen):
        for side, flag in ((0, far_right), (1, far_left)):

            @pl.when(flag == 0)
            def _(side=side):
                for f in chosen:
                    halo_copy(s, side, f, hemi).start()

    def send_early_far():
        for side in range(2):

            @pl.when(core == side)
            def _(side=side):
                for f in range(fields):
                    early_far_copy(f, side, side_now).start()

    def near_halo(s, wait):
        for side, flag in ((0, far_left), (1, far_right)) if wait == "wait_recv" else ((0, far_right), (1, far_left)):

            @pl.when(flag == 0)
            def _(side=side):
                for f in range(fields):
                    for hemi in range(2):
                        getattr(halo_copy(s, side, f, hemi), wait)()

    def far_wait(s):
        for f in range(fields):
            for hemi in range(2):
                halo_copy(s, 1, f, hemi, True).wait_recv()

    def each_level(s, hemi, action):
        for side, flags in ((0, (has_above, has_below)), (1, (has_below, has_above))):

            @pl.when(flags[1 if action == "wait_recv" else 0])
            def _(side=side):
                getattr(lev_copy(s, side, hemi), action)()

    def product(value, high, low):
        top, rest = split(value)
        out = jnp.dot(top, low[...], preferred_element_type=f32)
        out += jnp.dot(rest, high[...], preferred_element_type=f32)
        return out + jnp.dot(top, high[...], preferred_element_type=f32)

    spectral = (blocks + 1) * 2 * ROWS

    def spectra(s, f):
        for hemi in range(2):
            r = slice(hemi * ROWS, (hemi + 1) * ROWS)
            values = [state[s, f, r, n * LANES : (n + 1) * LANES] for n in range(blocks)]
            for k, (re, im) in padded_transform(values).items():
                at = (2 * k + hemi) * ROWS
                c, d = twist_ref[k : k + 1, :LANES], twist_ref[k : k + 1, LANES:]
                if k == 0:
                    out = (re, jnp.zeros_like(re))
                elif im is None:
                    out = (re * c, -re * d)
                else:
                    out = (re * c + im * d, im * c - re * d)
                spec_in[at : at + ROWS, :LANES] = out[0]
                spec_in[at : at + ROWS, LANES:] = out[1]
        gains = product(spec_in[...], fwd_hi, fwd_lo)
        sign = 1.0 if f == 0 else -1.0
        for k in range(blocks + 1):
            at = 2 * k * ROWS
            to = at + ROWS
            end = to + ROWS
            a = gains[at:to, :LANES] + sign * gains[to:end, :LANES]
            b = gains[at:to, LANES:] - sign * gains[to:end, LANES:]
            w = factor_ref[k : k + 1]
            pieces = (a * w[:, :LANES], b * w[:, LANES : 2 * LANES])
            turned[at:to, :LANES] = pieces[0]
            turned[at:to, LANES:] = pieces[1]
            turned[to:end, :LANES] = sign * pieces[0]
            turned[to:end, LANES:] = -sign * pieces[1]
            at, to, end = at + spectral, to + spectral, end + spectral
            pieces = (b * w[:, 2 * LANES : 3 * LANES], a * w[:, 3 * LANES :])
            turned[at:to, :LANES] = pieces[0]
            turned[at:to, LANES:] = pieces[1]
            turned[to:end, :LANES] = -sign * pieces[0]
            turned[to:end, LANES:] = sign * pieces[1]
        turned[...] = product(turned[...], inv_hi, inv_lo)
        for which, target in enumerate((smooth, slope)):
            for hemi in range(2):
                terms = {}
                for k in range(blocks + 1):
                    at = which * spectral + (2 * k + hemi) * ROWS
                    re, im = turned[at : at + ROWS, :LANES], turned[at : at + ROWS, LANES:]
                    c, d = twist_ref[k : k + 1, :LANES], twist_ref[k : k + 1, LANES:]
                    if k == 0:
                        terms[k] = (re, None)
                    elif k == blocks:
                        terms[k] = (re * c - im * d, None)
                    else:
                        terms[k] = (re * c - im * d, re * d + im * c)
                r = slice(hemi * ROWS, (hemi + 1) * ROWS)
                for n, value in enumerate(padded_inverse(terms, blocks)):
                    target[f, r, n * LANES : (n + 1) * LANES] = value

    def own_zonal(s):
        value = state[s].reshape(fields * 2 * ROWS, lat_count)
        zonal[...] = jnp.dot(own_ref[...], jnp.concatenate(split(value), 0), preferred_element_type=f32)

    def outer_zonal(value):
        value = value.reshape(fields * 2 * ROWS, lat_count)
        zonal[...] += jnp.dot(outer_ref[...], jnp.concatenate(split(value), 0), preferred_element_type=f32)

    def advance(s, hemi, target):
        r = slice(hemi * ROWS, (hemi + 1) * ROWS)
        for n in range(blocks):
            lanes = slice(n * LANES, (n + 1) * LANES)
            h, u, v = (state[s, f, r, lanes] for f in range(fields))
            secant, turn = line_ref[0:1, lanes], line_ref[1:2, lanes]
            zh, zu, zv = (
                zonal[(2 * f + hemi) * ROWS : (2 * f + hemi + 1) * ROWS, lanes] * secant for f in range(fields)
            )
            mh, mu, mv = (slope[f, r, lanes] for f in range(fields))
            vertical = levels[s, 0, r, lanes] + levels[s, 1, r, lanes] - 2.0 * h
            th = mixing * vertical - (u * zh + v * mh) - h * (zu + mv)
            tu = turn * v - (u * zu + v * mu) - zh
            tv = -(u * zv + v * mv) - mh - turn * u
            for f, t in enumerate((th, tu, tv)):
                target[f, r, lanes] = smooth[f, r, lanes] + courant * t

    count_here = 7 + crossing + has_below.astype(jnp.int32) + has_above.astype(jnp.int32)
    pl.semaphore_wait(barrier, count_here)
    for f in range(fields):
        for q in range(2):
            first_copy(q, f, side_now).start()

    for copy in loads:
        copy.wait()
    for s in range(STEPS):
        for f in range(fields):
            if s == 0:
                for hemi in range(2):
                    first_copy(core, f, hemi).wait_recv()
                    send_halo(0, hemi, (f,))
                if f == fields - 2:
                    send_early_far()
                if f == fields - 1:
                    for hemi in range(2):
                        each_level(0, hemi, "start")
            spectra(s, f)
        own_zonal(s)
        near_halo(s, "wait_recv")
        if s < STEPS - 1:

            @pl.when(crossing > 0)
            def _():
                far_wait(s)

            outer_zonal(halo[s] + far[s])
        else:
            outer_zonal(halo[s])
        for hemi in range(2):
            each_level(s, hemi, "wait_recv")
            target = state.at[s + 1]
            advance(s, hemi, target)
            if s < STEPS - 1:
                send_far(s + 1, hemi)
                send_halo(s + 1, hemi, range(fields))
                each_level(s + 1, hemi, "start")
                continue

            @pl.when(crossing == 0)
            def _(hemi=hemi):
                for f in range(fields):
                    last_copy(0, f, hemi, core, target, whole).start()

            @if_far
            def _(side, hemi=hemi):
                for f in range(fields):
                    last_copy(0, f, hemi, 1 - side, target, spans[side][0]).start()

    @pl.when(crossing > 0)
    def _():
        far_wait(STEPS - 1)
        outer_zonal(far[STEPS - 1])
        for hemi in range(2):
            advance(STEPS - 1, hemi, redo)

            @if_far
            def _(side, hemi=hemi):
                for f in range(fields):
                    last_copy(1, f, hemi, 1 - side, redo, spans[side][1]).start()

    target = state.at[STEPS]
    for side in range(2):

        @pl.when(core == side)
        def _(side=side):
            for f in range(fields):
                last_copy(0, f, 0, side, target, whole).wait_recv()
                last_copy(0, f, 0, 1 - side, target, spans[side][0]).wait_recv()
                last_copy(1, f, 0, 1 - side, redo, spans[side][1]).wait_recv()

    for f in range(fields):
        for q in range(2):
            first_copy(q, f, side_now).wait_send()
        early_far_copy(f, 0, side_now).wait_send()
    for hemi in range(2):

        @pl.when(crossing == 0)
        def _(hemi=hemi):
            for f in range(fields):
                last_copy(0, f, hemi, core, target, whole).wait_send()

        @if_far
        def _(side, hemi=hemi):
            for f in range(fields):
                for s in range(1, STEPS):
                    halo_copy(s, side, f, hemi, True).wait_send()
                last_copy(0, f, hemi, 1 - side, target, spans[side][0]).wait_send()
                last_copy(1, f, hemi, 1 - side, redo, spans[side][1]).wait_send()

        for s in range(STEPS):
            each_level(s, hemi, "wait_send")
    for s in range(STEPS):
        near_halo(s, "wait_send")


def body(sizes, thickness, wind_field):
    level_count, lon_count, lat_count = thickness.shape
    fields = 3
    blocks = lat_count // LANES
    spectral = (blocks + 1) * 2 * ROWS
    consts = tables(lat_count)
    hbm = pl.BlockSpec(memory_space=pltpu.HBM)
    vmem = pl.BlockSpec(memory_space=pltpu.VMEM)
    dma = pltpu.SemaphoreType.DMA
    return pl.pallas_call(
        functools.partial(kernel, sizes, [c.shape for c in consts]),
        out_shape=(
            pltpu.VMEM(thickness.shape, f32),
            pltpu.VMEM(wind_field.shape, f32),
        ),
        in_specs=[hbm, hbm] + [hbm] * len(consts),
        out_specs=(vmem, vmem),
        scratch_shapes=[pltpu.VMEM(c.shape, c.dtype) for c in consts]
        + [
            pltpu.VMEM((STEPS + 1, fields, lon_count, lat_count), f32),
            pltpu.VMEM((STEPS, fields, 2, ROWS, lat_count), f32),
            pltpu.VMEM((STEPS, fields, 2, ROWS, lat_count), f32),
            pltpu.VMEM((STEPS, 2, lon_count, lat_count), f32),
            pltpu.VMEM((spectral, 2 * LANES), f32),
            pltpu.VMEM((2 * spectral, 2 * LANES), f32),
            pltpu.VMEM((fields * lon_count, lat_count), f32),
            pltpu.VMEM((fields, lon_count, lat_count), f32),
            pltpu.VMEM((fields, lon_count, lat_count), f32),
            pltpu.VMEM((fields, lon_count, lat_count), f32),
            dma((len(consts),)),
            dma((2, fields)),
            dma((2, fields)),
            dma((STEPS, fields, 2)),
            dma((STEPS, fields, 2)),
            dma((STEPS, 2, fields, 2)),
            dma((STEPS, 2, fields, 2)),
            dma((STEPS, 2, 2)),
            dma((STEPS, 2, 2)),
            dma((2, 2, fields)),
            dma((2, 2, fields)),
        ],
        name="sphere_steps",
        compiler_params=pltpu.CompilerParams(collective_id=0, has_side_effects=True, vmem_limit_bytes=66_200_000),
    )(thickness, wind_field, *consts)


def solution(mesh):
    sizes = (mesh.shape["lon"], mesh.shape["lev"])
    in_specs = (P("lev", "lon", None), P(None, "lev", "lon", None))
    out_specs = (P("lev", "lon", None), P(None, "lev", "lon", None))
    return jax.shard_map(
        functools.partial(body, sizes), mesh=mesh, in_specs=in_specs, out_specs=out_specs, check_vma=False
    )
```

```python
import functools
import math

import jax
import jax.numpy as jnp
import numpy as np
from jax import lax
from jax.experimental import pallas as pl
from jax.experimental.pallas import tpu as pltpu
from jax.sharding import PartitionSpec as P

STEPS = 2
MESH = pl.DeviceIdType.MESH

courant = 0.2
mixing = 0.25
coriolis = 0.5
cos_floor = 0.25

LANES = 128
ROWS = 8
f32 = jnp.float32
bf16 = jnp.bfloat16


def rotate(z, angle):
    re, im = z
    c, s = math.cos(angle), math.sin(angle)
    if abs(s) < 1e-12:
        return (re, im) if c > 0 else (-re, -im)
    if abs(c) < 1e-12:
        return (-im, re) if s > 0 else (im, -re)
    return re * c - im * s, re * s + im * c


def complex_sum(values, sign):
    count = len(values)
    if count == 1:
        return values
    half = count // 2
    plus = [(a[0] + b[0], a[1] + b[1]) for a, b in zip(values[:half], values[half:])]
    minus = [(a[0] - b[0], a[1] - b[1]) for a, b in zip(values[:half], values[half:])]
    minus = [rotate(z, sign * 2 * math.pi * n / count) for n, z in enumerate(minus)]
    even, odd = complex_sum(plus, sign), complex_sum(minus, sign)
    return [z for pair in zip(even, odd) for z in pair]


def odd_frequencies(values):
    count = len(values)
    if count == 1:
        return {1: (values[0], None)}
    half = count // 2
    joined = [rotate((values[n], -values[n + half]), -math.pi * n / count) for n in range(half)]
    out = {}
    for t, (re, im) in enumerate(complex_sum(joined, -1)):
        k = 4 * t + 1
        if k <= count:
            out[k] = (re, im)
        else:
            out[2 * count - k] = (re, -im)
    return out


def real_transform(values):
    count = len(values)
    if count == 1:
        return {0: (values[0], None)}
    half = count // 2
    even = real_transform([values[n] + values[n + half] for n in range(half)])
    out = {2 * k: z for k, z in even.items()}
    out.update(odd_frequencies([values[n] - values[n + half] for n in range(half)]))
    return out


def padded_transform(values):
    out = {2 * k: z for k, z in real_transform(values).items()}
    out.update(odd_frequencies(values))
    return out


def odd_inverse(terms, count):
    if count == 1:
        return [terms[1][0]]
    half = count // 2
    joined = []
    for t in range(half):
        k = 4 * t + 1
        if k <= count:
            joined.append(terms[k])
        else:
            re, im = terms[2 * count - k]
            joined.append((re, -im))
    turned = [rotate(z, math.pi * n / count) for n, z in enumerate(complex_sum(joined, 1))]
    return [z[0] for z in turned] + [-z[1] for z in turned]


def real_inverse(terms, count):
    if count == 1:
        return [terms[0][0]]
    half = count // 2
    even = real_inverse({k // 2: z for k, z in terms.items() if k % 2 == 0}, half)
    odd = odd_inverse({k: z for k, z in terms.items() if k % 2}, half)
    return [a + b for a, b in zip(even, odd)] + [a - b for a, b in zip(even, odd)]


def padded_inverse(terms, count):
    even = real_inverse({k // 2: z for k, z in terms.items() if k % 2 == 0}, count)
    odd = odd_inverse({k: z for k, z in terms.items() if k % 2}, count)
    return [a + b for a, b in zip(even, odd)]


def split(value):
    high = value.astype(bf16)
    return high, (value - high.astype(f32)).astype(bf16)


def np_split(table):
    table = jnp.asarray(table.astype(np.float32))
    high = table.astype(bf16)
    return high, (table - high.astype(f32)).astype(bf16)


def tables(lat_count):
    length = 2 * lat_count
    blocks = lat_count // LANES
    ring = 2 * blocks
    kept = length // 3
    reach = kept // ring + 1
    lane = np.arange(LANES)
    shift = np.where(lane < 2 * reach, lane - reach, 0)
    valid = (lane < 2 * reach).astype(np.float64)
    psi = 2 * np.pi * (lane[:, None] + 0.5) * shift[None, :] / LANES
    cos, sin = np.cos(psi) * valid, np.sin(psi) * valid
    forward = np.block([[cos, sin], [sin, -cos]])
    inverse = np.block([[cos.T, sin.T], [sin.T, -cos.T]])
    small = np.arange(blocks + 1)
    phi = 2 * np.pi * small[:, None] * (lane[None, :] + 0.5) / length
    twist = np.concatenate([np.cos(phi), np.sin(phi)], 1)
    index = small[:, None] + ring * shift[None, :]
    weight = np.where((small == 0) | (small == blocks), 1.0, 2.0)[:, None] / length
    weight = weight * (np.abs(index) <= kept) * valid
    slope = weight * 2 * np.pi * index / length
    factor = np.concatenate([weight, weight, slope, -slope], 1)
    latitude = (np.arange(lat_count) + 0.5) * (np.pi / lat_count) - 0.5 * np.pi
    secant = 1.0 / np.maximum(np.cos(latitude), cos_floor)
    line = np.zeros((8, lat_count))
    line[0] = secant / 60.0
    line[1] = coriolis * np.sin(latitude)
    parts = 2 * 3
    own = np.zeros((parts * ROWS, parts * ROWS))
    outer = np.zeros((parts * ROWS, parts * ROWS))
    for part in range(parts):
        for row in range(ROWS):
            for offset, value in ((1, 45.0), (2, -9.0), (3, 1.0)):
                for sign in (1, -1):
                    at = row + sign * offset
                    target = own if 0 <= at < ROWS else outer
                    target[part * ROWS + row, part * ROWS + at % ROWS] = sign * value
    own = np.concatenate([own, own], 1)
    outer = np.concatenate([outer, outer], 1)
    return (
        *np_split(forward),
        *np_split(inverse),
        jnp.asarray(twist.astype(np.float32)),
        jnp.asarray(factor.astype(np.float32)),
        jnp.asarray(line.astype(np.float32)),
        jnp.asarray(own.astype(np.float32)).astype(bf16),
        jnp.asarray(outer.astype(np.float32)).astype(bf16),
    )


def kernel(sizes, const_shapes, thick_ref, wind_ref, *refs):
    count = len(const_shapes)
    const_hbm, (out_h, out_w), scratch = refs[:count], refs[count : count + 2], refs[count + 2 :]
    const_refs, scratch = scratch[:count], scratch[count:]
    fwd_hi, fwd_lo, inv_hi, inv_lo, twist_ref, factor_ref, line_ref, own_ref, outer_ref = const_refs
    (
        state, halo, far, levels, spec_in, turned, zonal, smooth, slope, redo, ahead, const_sem, first_send, first_recv,
        far_send, far_recv, halo_send, halo_recv, lev_send, lev_recv, last_send, last_recv,
    ) = scratch
    lon_size, lev_size = sizes
    fields, _, lat_count = state.shape[1:]
    blocks = lat_count // LANES
    half = lon_size // 2
    chips = half // 2
    depth = 2 * lev_size
    lon, lev = lax.axis_index("lon"), lax.axis_index("lev")
    side_now = lon // half
    chip = (lon % half) // 2
    core = lon % 2
    odd = chip % 2
    z = side_now * lev_size + lev

    there = (z + lev_size // 2 + lev_size * ((odd + core + side_now) % 2)) % depth

    def owner(q):
        return {"lon": (there // lev_size) * half + 2 * chip + q, "lev": there % lev_size}

    place = (z + depth - lev_size // 2) % depth
    level = place % lev_size
    held_by = (place // lev_size + odd) % 2

    def holder(hemi):
        return {"lon": hemi * half + 2 * chip + held_by, "lev": level}

    across = (1 - side_now) * half + 2 * chip
    after = side_now * half + 2 * ((chip + 1) % chips)
    before = side_now * half + 2 * ((chip + chips - 1) % chips) + 1
    right = (1 - core) * (lon + 1) + core * ((1 - held_by) * across + held_by * after)
    left = core * (lon - 1) + (1 - core) * (held_by * (across + 1) + (1 - held_by) * before)
    swap_right = core * held_by * (chip // (chips - 1))
    swap_left = (1 - core) * (1 - held_by) * ((chips - 1 - chip) // (chips - 1))
    has_below, has_above = level > 0, level < lev_size - 1
    far_right, far_left = core * (1 - held_by), (1 - core) * held_by
    crossing = far_right + far_left
    beyond = (there + lev_size) % depth
    far_owner = {"lon": (beyond // lev_size) * half + 2 * chip + core, "lev": beyond % lev_size}

    def far_holder(hemi):
        return {"lon": hemi * half + 2 * chip + 1 - held_by, "lev": level}

    def at_height(height):
        return {"lon": (height // lev_size) * half + 2 * chip + core, "lev": height % lev_size}

    upward, downward = at_height((z + 1) % depth), at_height((z + depth - 1) % depth)

    loads = [pltpu.make_async_copy(const_hbm[n], const_refs[n], const_sem.at[n]) for n in range(count)]
    for copy in loads:
        copy.start()
    halo[...] = jnp.zeros_like(halo)
    far[...] = jnp.zeros_like(far)

    @pl.when(jnp.logical_not(has_below))
    def _():
        for s in range(STEPS):
            levels[s, 0] = jnp.zeros_like(levels[s, 0])

    @pl.when(jnp.logical_not(has_above))
    def _():
        for s in range(STEPS):
            levels[s, 1] = jnp.zeros_like(levels[s, 1])

    barrier = pltpu.get_barrier_semaphore()
    for device in (owner(0), owner(1), holder(0), holder(1), far_owner):
        pl.semaphore_signal(barrier, inc=1, device_id=device, device_id_type=MESH)

    for at, flag in ((left, far_left), (right, far_right)):

        @pl.when(flag == 0)
        def _(at=at):
            pl.semaphore_signal(barrier, inc=1, device_id={"lon": at}, device_id_type=MESH)

    @pl.when(crossing > 0)
    def _():
        for hemi in range(2):
            pl.semaphore_signal(barrier, inc=1, device_id=far_holder(hemi), device_id_type=MESH)

    @pl.when(has_below)
    def _():
        pl.semaphore_signal(barrier, inc=1, device_id=downward, device_id_type=MESH)

    @pl.when(has_above)
    def _():
        pl.semaphore_signal(barrier, inc=1, device_id=upward, device_id_type=MESH)

    def rows(part):
        return pl.ds(pl.multiple_of(part * ROWS, ROWS), ROWS)

    def first_copy(q, f, hemi):
        at = rows(q)
        return pltpu.make_async_remote_copy(
            src_ref=thick_ref.at[0, at] if f == 0 else wind_ref.at[f - 1, 0, at], dst_ref=state.at[0, f, rows(hemi)],
            send_sem=first_send.at[q, f], recv_sem=first_recv.at[hemi, f],
            device_id=owner(q), device_id_type=MESH,
        )

    def early_far_copy(f, side, hemi):
        at = pl.ds(2 * ROWS - 3 if side == 0 else 0, 3)
        return pltpu.make_async_remote_copy(
            src_ref=thick_ref.at[0, at] if f == 0 else wind_ref.at[f - 1, 0, at],
            dst_ref=far.at[0, f, hemi, pl.ds(ROWS - 3 if side == 0 else 0, 3)],
            send_sem=far_send.at[0, f, 0], recv_sem=far_recv.at[0, f, hemi],
            device_id=far_owner, device_id_type=MESH,
        )

    def last_copy(part, f, hemi, q, origin, span):
        start, length = span
        source = origin.at[f, pl.ds(hemi * ROWS + start, length)]
        at = pl.ds(q * ROWS + start, length)
        return pltpu.make_async_remote_copy(
            src_ref=source, dst_ref=out_h.at[0, at] if f == 0 else out_w.at[f - 1, 0, at],
            send_sem=last_send.at[part, hemi, f], recv_sem=last_recv.at[part, q, f],
            device_id=holder(hemi), device_id_type=MESH,
        )

    def halo_copy(s, side, f, hemi, distant=False):
        start = ROWS - 3 if side == 0 else 0
        to = hemi if distant else (hemi + (swap_right if side == 0 else swap_left)) % 2
        send, recv = far_send.at[s, f, hemi], far_recv.at[s, f, hemi]
        if not distant:
            send, recv = halo_send.at[s, side, f, hemi], halo_recv.at[s, side, f, to]
        return pltpu.make_async_remote_copy(
            src_ref=(ahead.at[max(s - 1, 0)] if distant else state.at[s]).at[f, pl.ds(hemi * ROWS + start, 3)],
            dst_ref=(far if distant else halo).at[s, f, to, pl.ds(start, 3)],
            send_sem=send, recv_sem=recv,
            device_id={"lon": right if side == 0 else left}, device_id_type=MESH,
        )

    def lev_copy(s, side, hemi):
        return pltpu.make_async_remote_copy(
            src_ref=state.at[s, 0, rows(hemi)], dst_ref=levels.at[s, side, rows(hemi)],
            send_sem=lev_send.at[s, side, hemi], recv_sem=lev_recv.at[s, side, hemi],
            device_id=upward if side == 0 else downward, device_id_type=MESH,
        )

    whole, spans = (0, ROWS), {0: ((0, ROWS - 3), (ROWS - 3, 3)), 1: ((3, ROWS - 3), (0, 3))}

    def if_far(action):
        for side, flag in ((0, far_right), (1, far_left)):

            @pl.when(flag > 0)
            def _(side=side):
                action(side)

    def send_far(s, hemi):
        @if_far
        def _(side):
            for f in range(fields):
                halo_copy(s, side, f, hemi, True).start()

    def send_halo(s, hemi, chosen):
        for side, flag in ((0, far_right), (1, far_left)):

            @pl.when(flag == 0)
            def _(side=side):
                for f in chosen:
                    halo_copy(s, side, f, hemi).start()

    def near_halo(s, wait):
        for side, flag in ((0, far_left), (1, far_right)) if wait == "wait_recv" else ((0, far_right), (1, far_left)):

            @pl.when(flag == 0)
            def _(side=side):
                for f in range(fields):
                    for hemi in range(2):
                        getattr(halo_copy(s, side, f, hemi), wait)()

    def far_wait(s):
        for f in range(fields):
            for hemi in range(2):
                halo_copy(s, 1, f, hemi, True).wait_recv()

    def each_level(s, hemi, action):
        for side, flags in ((0, (has_above, has_below)), (1, (has_below, has_above))):

            @pl.when(flags[1 if action == "wait_recv" else 0])
            def _(side=side):
                getattr(lev_copy(s, side, hemi), action)()

    def product(value, high, low):
        top, rest = split(value)
        out = jnp.dot(top, low[...], preferred_element_type=f32)
        out += jnp.dot(rest, high[...], preferred_element_type=f32)
        return out + jnp.dot(top, high[...], preferred_element_type=f32)

    spectral = (blocks + 1) * 2 * ROWS

    def spectra(s, f):
        for hemi in range(2):
            r = slice(hemi * ROWS, (hemi + 1) * ROWS)
            values = [state[s, f, r, n * LANES : (n + 1) * LANES] for n in range(blocks)]
            for k, (re, im) in padded_transform(values).items():
                at = (2 * k + hemi) * ROWS
                c, d = twist_ref[k : k + 1, :LANES], twist_ref[k : k + 1, LANES:]
                if k == 0:
                    out = (re, jnp.zeros_like(re))
                elif im is None:
                    out = (re * c, -re * d)
                else:
                    out = (re * c + im * d, im * c - re * d)
                spec_in[at : at + ROWS, :LANES] = out[0]
                spec_in[at : at + ROWS, LANES:] = out[1]
        gains = product(spec_in[...], fwd_hi, fwd_lo)
        sign = 1.0 if f == 0 else -1.0
        for k in range(blocks + 1):
            at = 2 * k * ROWS
            to = at + ROWS
            end = to + ROWS
            a = gains[at:to, :LANES] + sign * gains[to:end, :LANES]
            b = gains[at:to, LANES:] - sign * gains[to:end, LANES:]
            w = factor_ref[k : k + 1]
            pieces = (a * w[:, :LANES], b * w[:, LANES : 2 * LANES])
            turned[at:to, :LANES] = pieces[0]
            turned[at:to, LANES:] = pieces[1]
            turned[to:end, :LANES] = sign * pieces[0]
            turned[to:end, LANES:] = -sign * pieces[1]
            at, to, end = at + spectral, to + spectral, end + spectral
            pieces = (b * w[:, 2 * LANES : 3 * LANES], a * w[:, 3 * LANES :])
            turned[at:to, :LANES] = pieces[0]
            turned[at:to, LANES:] = pieces[1]
            turned[to:end, :LANES] = -sign * pieces[0]
            turned[to:end, LANES:] = sign * pieces[1]
        turned[...] = product(turned[...], inv_hi, inv_lo)
        for which, target in enumerate((smooth, slope)):
            for hemi in range(2):
                terms = {}
                for k in range(blocks + 1):
                    at = which * spectral + (2 * k + hemi) * ROWS
                    re, im = turned[at : at + ROWS, :LANES], turned[at : at + ROWS, LANES:]
                    c, d = twist_ref[k : k + 1, :LANES], twist_ref[k : k + 1, LANES:]
                    if k == 0:
                        terms[k] = (re, None)
                    elif k == blocks:
                        terms[k] = (re * c - im * d, None)
                    else:
                        terms[k] = (re * c - im * d, re * d + im * c)
                r = slice(hemi * ROWS, (hemi + 1) * ROWS)
                for n, value in enumerate(padded_inverse(terms, blocks)):
                    target[f, r, n * LANES : (n + 1) * LANES] = value

    def own_zonal(s):
        value = state[s].reshape(fields * 2 * ROWS, lat_count)
        zonal[...] = jnp.dot(own_ref[...], jnp.concatenate(split(value), 0), preferred_element_type=f32)

    def outer_zonal(value):
        value = value.reshape(fields * 2 * ROWS, lat_count)
        zonal[...] += jnp.dot(outer_ref[...], jnp.concatenate(split(value), 0), preferred_element_type=f32)

    def advance(s, hemi, target):
        r = slice(hemi * ROWS, (hemi + 1) * ROWS)
        for n in range(blocks):
            lanes = slice(n * LANES, (n + 1) * LANES)
            h, u, v = (state[s, f, r, lanes] for f in range(fields))
            secant, turn = line_ref[0:1, lanes], line_ref[1:2, lanes]
            zh, zu, zv = (
                zonal[(2 * f + hemi) * ROWS : (2 * f + hemi + 1) * ROWS, lanes] * secant for f in range(fields)
            )
            mh, mu, mv = (slope[f, r, lanes] for f in range(fields))
            vertical = levels[s, 0, r, lanes] + levels[s, 1, r, lanes] - 2.0 * h
            th = mixing * vertical - (u * zh + v * mh) - h * (zu + mv)
            tu = turn * v - (u * zu + v * mu) - zh
            tv = -(u * zv + v * mv) - mh - turn * u
            for f, t in enumerate((th, tu, tv)):
                target[f, r, lanes] = smooth[f, r, lanes] + courant * t

    count_here = 7 + crossing + has_below.astype(jnp.int32) + has_above.astype(jnp.int32)
    pl.semaphore_wait(barrier, count_here)
    for f in range(fields):
        for q in range(2):
            first_copy(q, f, side_now).start()
        for side in range(2):

            @pl.when(core == side)
            def _(side=side):
                early_far_copy(f, side, side_now).start()

    for copy in loads:
        copy.wait()
    for s in range(STEPS):
        for f in range(fields):
            if s == 0:
                for hemi in range(2):
                    first_copy(core, f, hemi).wait_recv()
                    if f == 0:
                        each_level(0, hemi, "start")
                    send_halo(0, hemi, (f,))
            spectra(s, f)
        own_zonal(s)
        if s < STEPS - 1:
            for hemi in range(2):
                each_level(s, hemi, "wait_recv")

            @pl.when(crossing > 0)
            def _():
                far_wait(s)
                outer_zonal(far[s])
                for hemi in range(2):
                    advance(s, hemi, ahead.at[s])
                    send_far(s + 1, hemi)

        near_halo(s, "wait_recv")
        outer_zonal(halo[s])
        for hemi in range(2):
            if s == STEPS - 1:
                each_level(s, hemi, "wait_recv")
            target = state.at[s + 1]
            advance(s, hemi, target)
            if s < STEPS - 1:
                send_halo(s + 1, hemi, range(fields))
                each_level(s + 1, hemi, "start")
                continue

            @pl.when(crossing == 0)
            def _(hemi=hemi):
                for f in range(fields):
                    last_copy(0, f, hemi, core, target, whole).start()

            @if_far
            def _(side, hemi=hemi):
                for f in range(fields):
                    last_copy(0, f, hemi, 1 - side, target, spans[side][0]).start()

    @pl.when(crossing > 0)
    def _():
        far_wait(STEPS - 1)
        outer_zonal(far[STEPS - 1])
        for hemi in range(2):
            advance(STEPS - 1, hemi, redo)

            @if_far
            def _(side, hemi=hemi):
                for f in range(fields):
                    last_copy(1, f, hemi, 1 - side, redo, spans[side][1]).start()

    target = state.at[STEPS]
    for side in range(2):

        @pl.when(core == side)
        def _(side=side):
            for f in range(fields):
                last_copy(0, f, 0, side, target, whole).wait_recv()
                last_copy(0, f, 0, 1 - side, target, spans[side][0]).wait_recv()
                last_copy(1, f, 0, 1 - side, redo, spans[side][1]).wait_recv()

    for f in range(fields):
        for q in range(2):
            first_copy(q, f, side_now).wait_send()
        early_far_copy(f, 0, side_now).wait_send()
    for hemi in range(2):

        @pl.when(crossing == 0)
        def _(hemi=hemi):
            for f in range(fields):
                last_copy(0, f, hemi, core, target, whole).wait_send()

        @if_far
        def _(side, hemi=hemi):
            for f in range(fields):
                for s in range(1, STEPS):
                    halo_copy(s, side, f, hemi, True).wait_send()
                last_copy(0, f, hemi, 1 - side, target, spans[side][0]).wait_send()
                last_copy(1, f, hemi, 1 - side, redo, spans[side][1]).wait_send()

        for s in range(STEPS):
            each_level(s, hemi, "wait_send")
    for s in range(STEPS):
        near_halo(s, "wait_send")


def body(sizes, thickness, wind_field):
    level_count, lon_count, lat_count = thickness.shape
    fields = 3
    blocks = lat_count // LANES
    spectral = (blocks + 1) * 2 * ROWS
    consts = tables(lat_count)
    hbm = pl.BlockSpec(memory_space=pltpu.HBM)
    vmem = pl.BlockSpec(memory_space=pltpu.VMEM)
    dma = pltpu.SemaphoreType.DMA
    return pl.pallas_call(
        functools.partial(kernel, sizes, [c.shape for c in consts]),
        out_shape=(
            pltpu.VMEM(thickness.shape, f32),
            pltpu.VMEM(wind_field.shape, f32),
        ),
        in_specs=[hbm, hbm] + [hbm] * len(consts),
        out_specs=(vmem, vmem),
        scratch_shapes=[pltpu.VMEM(c.shape, c.dtype) for c in consts]
        + [
            pltpu.VMEM((STEPS + 1, fields, lon_count, lat_count), f32),
            pltpu.VMEM((STEPS, fields, 2, ROWS, lat_count), f32),
            pltpu.VMEM((STEPS, fields, 2, ROWS, lat_count), f32),
            pltpu.VMEM((STEPS, 2, lon_count, lat_count), f32),
            pltpu.VMEM((spectral, 2 * LANES), f32),
            pltpu.VMEM((2 * spectral, 2 * LANES), f32),
            pltpu.VMEM((fields * lon_count, lat_count), f32),
            pltpu.VMEM((fields, lon_count, lat_count), f32),
            pltpu.VMEM((fields, lon_count, lat_count), f32),
            pltpu.VMEM((fields, lon_count, lat_count), f32),
            pltpu.VMEM((STEPS - 1, fields, lon_count, lat_count), f32),
            dma((len(consts),)),
            dma((2, fields)),
            dma((2, fields)),
            dma((STEPS, fields, 2)),
            dma((STEPS, fields, 2)),
            dma((STEPS, 2, fields, 2)),
            dma((STEPS, 2, fields, 2)),
            dma((STEPS, 2, 2)),
            dma((STEPS, 2, 2)),
            dma((2, 2, fields)),
            dma((2, 2, fields)),
        ],
        name="sphere_steps",
        compiler_params=pltpu.CompilerParams(collective_id=0, has_side_effects=True, vmem_limit_bytes=66_200_000),
    )(thickness, wind_field, *consts)


def solution(mesh):
    sizes = (mesh.shape["lon"], mesh.shape["lev"])
    in_specs = (P("lev", "lon", None), P(None, "lev", "lon", None))
    out_specs = (P("lev", "lon", None), P(None, "lev", "lon", None))
    return jax.shard_map(
        functools.partial(body, sizes), mesh=mesh, in_specs=in_specs, out_specs=out_specs, check_vma=False
    )
```

```python
import functools
import math

import jax
import jax.numpy as jnp
import numpy as np
from jax import lax
from jax.experimental import pallas as pl
from jax.experimental.pallas import tpu as pltpu
from jax.sharding import PartitionSpec as P

STEPS = 2
MESH = pl.DeviceIdType.MESH

courant = 0.2
mixing = 0.25
coriolis = 0.5
cos_floor = 0.25

LANES = 128
ROWS = 8
f32 = jnp.float32
bf16 = jnp.bfloat16


def rotate(z, angle):
    re, im = z
    c, s = math.cos(angle), math.sin(angle)
    if abs(s) < 1e-12:
        return (re, im) if c > 0 else (-re, -im)
    if abs(c) < 1e-12:
        return (-im, re) if s > 0 else (im, -re)
    return re * c - im * s, re * s + im * c


def complex_sum(values, sign):
    count = len(values)
    if count == 1:
        return values
    half = count // 2
    plus = [(a[0] + b[0], a[1] + b[1]) for a, b in zip(values[:half], values[half:])]
    minus = [(a[0] - b[0], a[1] - b[1]) for a, b in zip(values[:half], values[half:])]
    minus = [rotate(z, sign * 2 * math.pi * n / count) for n, z in enumerate(minus)]
    even, odd = complex_sum(plus, sign), complex_sum(minus, sign)
    return [z for pair in zip(even, odd) for z in pair]


def odd_frequencies(values):
    count = len(values)
    if count == 1:
        return {1: (values[0], None)}
    half = count // 2
    joined = [rotate((values[n], -values[n + half]), -math.pi * n / count) for n in range(half)]
    out = {}
    for t, (re, im) in enumerate(complex_sum(joined, -1)):
        k = 4 * t + 1
        if k <= count:
            out[k] = (re, im)
        else:
            out[2 * count - k] = (re, -im)
    return out


def real_transform(values):
    count = len(values)
    if count == 1:
        return {0: (values[0], None)}
    half = count // 2
    even = real_transform([values[n] + values[n + half] for n in range(half)])
    out = {2 * k: z for k, z in even.items()}
    out.update(odd_frequencies([values[n] - values[n + half] for n in range(half)]))
    return out


def padded_transform(values):
    out = {2 * k: z for k, z in real_transform(values).items()}
    out.update(odd_frequencies(values))
    return out


def odd_inverse(terms, count):
    if count == 1:
        return [terms[1][0]]
    half = count // 2
    joined = []
    for t in range(half):
        k = 4 * t + 1
        if k <= count:
            joined.append(terms[k])
        else:
            re, im = terms[2 * count - k]
            joined.append((re, -im))
    turned = [rotate(z, math.pi * n / count) for n, z in enumerate(complex_sum(joined, 1))]
    return [z[0] for z in turned] + [-z[1] for z in turned]


def real_inverse(terms, count):
    if count == 1:
        return [terms[0][0]]
    half = count // 2
    even = real_inverse({k // 2: z for k, z in terms.items() if k % 2 == 0}, half)
    odd = odd_inverse({k: z for k, z in terms.items() if k % 2}, half)
    return [a + b for a, b in zip(even, odd)] + [a - b for a, b in zip(even, odd)]


def padded_inverse(terms, count):
    even = real_inverse({k // 2: z for k, z in terms.items() if k % 2 == 0}, count)
    odd = odd_inverse({k: z for k, z in terms.items() if k % 2}, count)
    return [a + b for a, b in zip(even, odd)]


def split(value):
    high = value.astype(bf16)
    return high, (value - high.astype(f32)).astype(bf16)


def np_split(table):
    table = jnp.asarray(table.astype(np.float32))
    high = table.astype(bf16)
    return high, (table - high.astype(f32)).astype(bf16)


def tables(lat_count):
    length = 2 * lat_count
    blocks = lat_count // LANES
    ring = 2 * blocks
    kept = length // 3
    reach = kept // ring + 1
    lane = np.arange(LANES)
    shift = np.where(lane < 2 * reach, lane - reach, 0)
    valid = (lane < 2 * reach).astype(np.float64)
    psi = 2 * np.pi * (lane[:, None] + 0.5) * shift[None, :] / LANES
    cos, sin = np.cos(psi) * valid, np.sin(psi) * valid
    forward = np.block([[cos, sin], [sin, -cos]])
    inverse = np.block([[cos.T, sin.T], [sin.T, -cos.T]])
    small = np.arange(blocks + 1)
    phi = 2 * np.pi * small[:, None] * (lane[None, :] + 0.5) / length
    twist = np.concatenate([np.cos(phi), np.sin(phi)], 1)
    index = small[:, None] + ring * shift[None, :]
    weight = np.where((small == 0) | (small == blocks), 1.0, 2.0)[:, None] / length
    weight = weight * (np.abs(index) <= kept) * valid
    slope = weight * 2 * np.pi * index / length
    factor = np.concatenate([weight, weight, slope, -slope], 1)
    latitude = (np.arange(lat_count) + 0.5) * (np.pi / lat_count) - 0.5 * np.pi
    secant = 1.0 / np.maximum(np.cos(latitude), cos_floor)
    line = np.zeros((8, lat_count))
    line[0] = secant / 60.0
    line[1] = coriolis * np.sin(latitude)
    parts = 2 * 3
    own = np.zeros((parts * ROWS, parts * ROWS))
    outer = np.zeros((parts * ROWS, parts * ROWS))
    for part in range(parts):
        for row in range(ROWS):
            for offset, value in ((1, 45.0), (2, -9.0), (3, 1.0)):
                for sign in (1, -1):
                    at = row + sign * offset
                    target = own if 0 <= at < ROWS else outer
                    target[part * ROWS + row, part * ROWS + at % ROWS] = sign * value
    own = np.concatenate([own, own], 1)
    outer = np.concatenate([outer, outer], 1)
    return (
        *np_split(forward),
        *np_split(inverse),
        jnp.asarray(twist.astype(np.float32)),
        jnp.asarray(factor.astype(np.float32)),
        jnp.asarray(line.astype(np.float32)),
        jnp.asarray(own.astype(np.float32)).astype(bf16),
        jnp.asarray(outer.astype(np.float32)).astype(bf16),
    )


def kernel(sizes, const_shapes, thick_ref, wind_ref, *refs):
    count = len(const_shapes)
    const_hbm, (out_h, out_w), scratch = refs[:count], refs[count : count + 2], refs[count + 2 :]
    const_refs, scratch = scratch[:count], scratch[count:]
    fwd_hi, fwd_lo, inv_hi, inv_lo, twist_ref, factor_ref, line_ref, own_ref, outer_ref = const_refs
    (
        state, halo, far, levels, spec_in, turned, zonal, smooth, slope, redo, ahead, const_sem, first_send, first_recv,
        far_send, far_recv, halo_send, halo_recv, lev_send, lev_recv, last_send, last_recv,
    ) = scratch
    lon_size, lev_size = sizes
    fields, _, lat_count = state.shape[1:]
    blocks = lat_count // LANES
    half = lon_size // 2
    chips = half // 2
    depth = 2 * lev_size
    lon, lev = lax.axis_index("lon"), lax.axis_index("lev")
    side_now = lon // half
    chip = (lon % half) // 2
    core = lon % 2
    odd = chip % 2
    z = side_now * lev_size + lev

    there = (z + lev_size // 2 + lev_size * ((odd + core + side_now) % 2)) % depth

    def owner(q):
        return {"lon": (there // lev_size) * half + 2 * chip + q, "lev": there % lev_size}

    place = (z + depth - lev_size // 2) % depth
    level = place % lev_size
    held_by = (place // lev_size + odd) % 2

    def holder(hemi):
        return {"lon": hemi * half + 2 * chip + held_by, "lev": level}

    across = (1 - side_now) * half + 2 * chip
    after = side_now * half + 2 * ((chip + 1) % chips)
    before = side_now * half + 2 * ((chip + chips - 1) % chips) + 1
    right = (1 - core) * (lon + 1) + core * ((1 - held_by) * across + held_by * after)
    left = core * (lon - 1) + (1 - core) * (held_by * (across + 1) + (1 - held_by) * before)
    swap_right = core * held_by * (chip // (chips - 1))
    swap_left = (1 - core) * (1 - held_by) * ((chips - 1 - chip) // (chips - 1))
    has_below, has_above = level > 0, level < lev_size - 1
    far_right, far_left = core * (1 - held_by), (1 - core) * held_by
    crossing = far_right + far_left
    beyond = (there + lev_size) % depth
    far_owner = {"lon": (beyond // lev_size) * half + 2 * chip + core, "lev": beyond % lev_size}

    def far_holder(hemi):
        return {"lon": hemi * half + 2 * chip + 1 - held_by, "lev": level}

    def at_height(height):
        return {"lon": (height // lev_size) * half + 2 * chip + core, "lev": height % lev_size}

    upward, downward = at_height((z + 1) % depth), at_height((z + depth - 1) % depth)

    loads = [pltpu.make_async_copy(const_hbm[n], const_refs[n], const_sem.at[n]) for n in range(count)]
    for copy in loads:
        copy.start()
    halo[...] = jnp.zeros_like(halo)
    far[...] = jnp.zeros_like(far)

    @pl.when(jnp.logical_not(has_below))
    def _():
        for s in range(STEPS):
            levels[s, 0] = jnp.zeros_like(levels[s, 0])

    @pl.when(jnp.logical_not(has_above))
    def _():
        for s in range(STEPS):
            levels[s, 1] = jnp.zeros_like(levels[s, 1])

    barrier = pltpu.get_barrier_semaphore()
    for device in (owner(0), owner(1), holder(0), holder(1), far_owner):
        pl.semaphore_signal(barrier, inc=1, device_id=device, device_id_type=MESH)

    for at, flag in ((left, far_left), (right, far_right)):

        @pl.when(flag == 0)
        def _(at=at):
            pl.semaphore_signal(barrier, inc=1, device_id={"lon": at}, device_id_type=MESH)

    @pl.when(crossing > 0)
    def _():
        for hemi in range(2):
            pl.semaphore_signal(barrier, inc=1, device_id=far_holder(hemi), device_id_type=MESH)

    @pl.when(has_below)
    def _():
        pl.semaphore_signal(barrier, inc=1, device_id=downward, device_id_type=MESH)

    @pl.when(has_above)
    def _():
        pl.semaphore_signal(barrier, inc=1, device_id=upward, device_id_type=MESH)

    def rows(part):
        return pl.ds(pl.multiple_of(part * ROWS, ROWS), ROWS)

    def first_copy(q, f, hemi):
        at = rows(q)
        return pltpu.make_async_remote_copy(
            src_ref=thick_ref.at[0, at] if f == 0 else wind_ref.at[f - 1, 0, at], dst_ref=state.at[0, f, rows(hemi)],
            send_sem=first_send.at[q, f], recv_sem=first_recv.at[hemi, f],
            device_id=owner(q), device_id_type=MESH,
        )

    def early_far_copy(f, side, hemi):
        at = pl.ds(2 * ROWS - 3 if side == 0 else 0, 3)
        return pltpu.make_async_remote_copy(
            src_ref=thick_ref.at[0, at] if f == 0 else wind_ref.at[f - 1, 0, at],
            dst_ref=far.at[0, f, hemi, pl.ds(ROWS - 3 if side == 0 else 0, 3)],
            send_sem=far_send.at[0, f, 0], recv_sem=far_recv.at[0, f, hemi],
            device_id=far_owner, device_id_type=MESH,
        )

    def last_copy(part, f, hemi, q, origin, span):
        start, length = span
        source = origin.at[f, pl.ds(hemi * ROWS + start, length)]
        at = pl.ds(q * ROWS + start, length)
        return pltpu.make_async_remote_copy(
            src_ref=source, dst_ref=out_h.at[0, at] if f == 0 else out_w.at[f - 1, 0, at],
            send_sem=last_send.at[part, hemi, f], recv_sem=last_recv.at[part, q, f],
            device_id=holder(hemi), device_id_type=MESH,
        )

    def halo_copy(s, side, f, hemi, distant=False):
        start = ROWS - 3 if side == 0 else 0
        to = hemi if distant else (hemi + (swap_right if side == 0 else swap_left)) % 2
        send, recv = far_send.at[s, f, hemi], far_recv.at[s, f, hemi]
        if not distant:
            send, recv = halo_send.at[s, side, f, hemi], halo_recv.at[s, side, f, to]
        return pltpu.make_async_remote_copy(
            src_ref=(ahead.at[max(s - 1, 0)] if distant else state.at[s]).at[f, pl.ds(hemi * ROWS + start, 3)],
            dst_ref=(far if distant else halo).at[s, f, to, pl.ds(start, 3)],
            send_sem=send, recv_sem=recv,
            device_id={"lon": right if side == 0 else left}, device_id_type=MESH,
        )

    def lev_copy(s, side, hemi):
        return pltpu.make_async_remote_copy(
            src_ref=state.at[s, 0, rows(hemi)], dst_ref=levels.at[s, side, rows(hemi)],
            send_sem=lev_send.at[s, side, hemi], recv_sem=lev_recv.at[s, side, hemi],
            device_id=upward if side == 0 else downward, device_id_type=MESH,
        )

    whole, spans = (0, ROWS), {0: ((0, ROWS - 3), (ROWS - 3, 3)), 1: ((3, ROWS - 3), (0, 3))}

    def if_far(action):
        for side, flag in ((0, far_right), (1, far_left)):

            @pl.when(flag > 0)
            def _(side=side):
                action(side)

    def send_far(s, hemi):
        @if_far
        def _(side):
            for f in range(fields):
                halo_copy(s, side, f, hemi, True).start()

    def send_halo(s, hemi, chosen):
        for side, flag in ((0, far_right), (1, far_left)):

            @pl.when(flag == 0)
            def _(side=side):
                for f in chosen:
                    halo_copy(s, side, f, hemi).start()

    def near_halo(s, wait):
        for side, flag in ((0, far_left), (1, far_right)) if wait == "wait_recv" else ((0, far_right), (1, far_left)):

            @pl.when(flag == 0)
            def _(side=side):
                for f in range(fields):
                    for hemi in range(2):
                        getattr(halo_copy(s, side, f, hemi), wait)()

    def far_wait(s):
        for f in range(fields):
            for hemi in range(2):
                halo_copy(s, 1, f, hemi, True).wait_recv()

    def each_level(s, hemi, action):
        for side, flags in ((0, (has_above, has_below)), (1, (has_below, has_above))):

            @pl.when(flags[1 if action == "wait_recv" else 0])
            def _(side=side):
                getattr(lev_copy(s, side, hemi), action)()

    def product(value, high, low):
        top, rest = split(value)
        out = jnp.dot(top, low[...], preferred_element_type=f32)
        out += jnp.dot(rest, high[...], preferred_element_type=f32)
        return out + jnp.dot(top, high[...], preferred_element_type=f32)

    spectral = (blocks + 1) * 2 * ROWS

    def spectra(s, f):
        for hemi in range(2):
            r = slice(hemi * ROWS, (hemi + 1) * ROWS)
            values = [state[s, f, r, n * LANES : (n + 1) * LANES] for n in range(blocks)]
            for k, (re, im) in padded_transform(values).items():
                at = (2 * k + hemi) * ROWS
                c, d = twist_ref[k : k + 1, :LANES], twist_ref[k : k + 1, LANES:]
                if k == 0:
                    out = (re, jnp.zeros_like(re))
                elif im is None:
                    out = (re * c, -re * d)
                else:
                    out = (re * c + im * d, im * c - re * d)
                spec_in[at : at + ROWS, :LANES] = out[0]
                spec_in[at : at + ROWS, LANES:] = out[1]
        gains = product(spec_in[...], fwd_hi, fwd_lo)
        sign = 1.0 if f == 0 else -1.0
        for k in range(blocks + 1):
            at = 2 * k * ROWS
            to = at + ROWS
            end = to + ROWS
            a = gains[at:to, :LANES] + sign * gains[to:end, :LANES]
            b = gains[at:to, LANES:] - sign * gains[to:end, LANES:]
            w = factor_ref[k : k + 1]
            pieces = (a * w[:, :LANES], b * w[:, LANES : 2 * LANES])
            turned[at:to, :LANES] = pieces[0]
            turned[at:to, LANES:] = pieces[1]
            turned[to:end, :LANES] = sign * pieces[0]
            turned[to:end, LANES:] = -sign * pieces[1]
            at, to, end = at + spectral, to + spectral, end + spectral
            pieces = (b * w[:, 2 * LANES : 3 * LANES], a * w[:, 3 * LANES :])
            turned[at:to, :LANES] = pieces[0]
            turned[at:to, LANES:] = pieces[1]
            turned[to:end, :LANES] = -sign * pieces[0]
            turned[to:end, LANES:] = sign * pieces[1]
        turned[...] = product(turned[...], inv_hi, inv_lo)
        for which, target in enumerate((smooth, slope)):
            for hemi in range(2):
                terms = {}
                for k in range(blocks + 1):
                    at = which * spectral + (2 * k + hemi) * ROWS
                    re, im = turned[at : at + ROWS, :LANES], turned[at : at + ROWS, LANES:]
                    c, d = twist_ref[k : k + 1, :LANES], twist_ref[k : k + 1, LANES:]
                    if k == 0:
                        terms[k] = (re, None)
                    elif k == blocks:
                        terms[k] = (re * c - im * d, None)
                    else:
                        terms[k] = (re * c - im * d, re * d + im * c)
                r = slice(hemi * ROWS, (hemi + 1) * ROWS)
                for n, value in enumerate(padded_inverse(terms, blocks)):
                    target[f, r, n * LANES : (n + 1) * LANES] = value

    def own_zonal(s):
        value = state[s].reshape(fields * 2 * ROWS, lat_count)
        zonal[...] = jnp.dot(own_ref[...], jnp.concatenate(split(value), 0), preferred_element_type=f32)

    def outer_zonal(value):
        value = value.reshape(fields * 2 * ROWS, lat_count)
        zonal[...] += jnp.dot(outer_ref[...], jnp.concatenate(split(value), 0), preferred_element_type=f32)

    def advance(s, hemi, target):
        r = slice(hemi * ROWS, (hemi + 1) * ROWS)
        for n in range(blocks):
            lanes = slice(n * LANES, (n + 1) * LANES)
            h, u, v = (state[s, f, r, lanes] for f in range(fields))
            secant, turn = line_ref[0:1, lanes], line_ref[1:2, lanes]
            zh, zu, zv = (
                zonal[(2 * f + hemi) * ROWS : (2 * f + hemi + 1) * ROWS, lanes] * secant for f in range(fields)
            )
            mh, mu, mv = (slope[f, r, lanes] for f in range(fields))
            vertical = levels[s, 0, r, lanes] + levels[s, 1, r, lanes] - 2.0 * h
            th = mixing * vertical - (u * zh + v * mh) - h * (zu + mv)
            tu = turn * v - (u * zu + v * mu) - zh
            tv = -(u * zv + v * mv) - mh - turn * u
            for f, t in enumerate((th, tu, tv)):
                target[f, r, lanes] = smooth[f, r, lanes] + courant * t

    count_here = 7 + crossing + has_below.astype(jnp.int32) + has_above.astype(jnp.int32)
    pl.semaphore_wait(barrier, count_here)
    for f in range(fields):
        for q in range(2):
            first_copy(q, f, side_now).start()
        for side in range(2):

            @pl.when(core == side)
            def _(side=side):
                early_far_copy(f, side, side_now).start()

    for copy in loads:
        copy.wait()
    for s in range(STEPS):
        for f in range(fields):
            if s == 0:
                for hemi in range(2):
                    first_copy(core, f, hemi).wait_recv()
                    if f == 0:
                        each_level(0, hemi, "start")
                    send_halo(0, hemi, (f,))
            spectra(s, f)
        own_zonal(s)
        if s < STEPS - 1:
            for hemi in range(2):
                each_level(s, hemi, "wait_recv")

            @pl.when(crossing > 0)
            def _():
                far_wait(s)
                outer_zonal(far[s])
                for hemi in range(2):
                    advance(s, hemi, ahead.at[s])
                    send_far(s + 1, hemi)

        near_halo(s, "wait_recv")
        outer_zonal(halo[s])
        for hemi in range(2):
            if s == STEPS - 1:
                each_level(s, hemi, "wait_recv")
            target = state.at[s + 1]
            advance(s, hemi, target)
            if s < STEPS - 1:
                each_level(s + 1, hemi, "start")
                send_halo(s + 1, hemi, range(fields))
                continue

            @pl.when(crossing == 0)
            def _(hemi=hemi):
                for f in range(fields):
                    last_copy(0, f, hemi, core, target, whole).start()

            @if_far
            def _(side, hemi=hemi):
                for f in range(fields):
                    last_copy(0, f, hemi, 1 - side, target, spans[side][0]).start()

    @pl.when(crossing > 0)
    def _():
        far_wait(STEPS - 1)
        outer_zonal(far[STEPS - 1])
        for hemi in range(2):
            advance(STEPS - 1, hemi, redo)

            @if_far
            def _(side, hemi=hemi):
                for f in range(fields):
                    last_copy(1, f, hemi, 1 - side, redo, spans[side][1]).start()

    target = state.at[STEPS]
    for side in range(2):

        @pl.when(core == side)
        def _(side=side):
            for f in range(fields):
                last_copy(0, f, 0, side, target, whole).wait_recv()
                last_copy(0, f, 0, 1 - side, target, spans[side][0]).wait_recv()
                last_copy(1, f, 0, 1 - side, redo, spans[side][1]).wait_recv()

    for f in range(fields):
        for q in range(2):
            first_copy(q, f, side_now).wait_send()
        early_far_copy(f, 0, side_now).wait_send()
    for hemi in range(2):

        @pl.when(crossing == 0)
        def _(hemi=hemi):
            for f in range(fields):
                last_copy(0, f, hemi, core, target, whole).wait_send()

        @if_far
        def _(side, hemi=hemi):
            for f in range(fields):
                for s in range(1, STEPS):
                    halo_copy(s, side, f, hemi, True).wait_send()
                last_copy(0, f, hemi, 1 - side, target, spans[side][0]).wait_send()
                last_copy(1, f, hemi, 1 - side, redo, spans[side][1]).wait_send()

        for s in range(STEPS):
            each_level(s, hemi, "wait_send")
    for s in range(STEPS):
        near_halo(s, "wait_send")


def body(sizes, thickness, wind_field):
    level_count, lon_count, lat_count = thickness.shape
    fields = 3
    blocks = lat_count // LANES
    spectral = (blocks + 1) * 2 * ROWS
    consts = tables(lat_count)
    hbm = pl.BlockSpec(memory_space=pltpu.HBM)
    vmem = pl.BlockSpec(memory_space=pltpu.VMEM)
    dma = pltpu.SemaphoreType.DMA
    return pl.pallas_call(
        functools.partial(kernel, sizes, [c.shape for c in consts]),
        out_shape=(
            pltpu.VMEM(thickness.shape, f32),
            pltpu.VMEM(wind_field.shape, f32),
        ),
        in_specs=[hbm, hbm] + [hbm] * len(consts),
        out_specs=(vmem, vmem),
        scratch_shapes=[pltpu.VMEM(c.shape, c.dtype) for c in consts]
        + [
            pltpu.VMEM((STEPS + 1, fields, lon_count, lat_count), f32),
            pltpu.VMEM((STEPS, fields, 2, ROWS, lat_count), f32),
            pltpu.VMEM((STEPS, fields, 2, ROWS, lat_count), f32),
            pltpu.VMEM((STEPS, 2, lon_count, lat_count), f32),
            pltpu.VMEM((spectral, 2 * LANES), f32),
            pltpu.VMEM((2 * spectral, 2 * LANES), f32),
            pltpu.VMEM((fields * lon_count, lat_count), f32),
            pltpu.VMEM((fields, lon_count, lat_count), f32),
            pltpu.VMEM((fields, lon_count, lat_count), f32),
            pltpu.VMEM((fields, lon_count, lat_count), f32),
            pltpu.VMEM((STEPS - 1, fields, lon_count, lat_count), f32),
            dma((len(consts),)),
            dma((2, fields)),
            dma((2, fields)),
            dma((STEPS, fields, 2)),
            dma((STEPS, fields, 2)),
            dma((STEPS, 2, fields, 2)),
            dma((STEPS, 2, fields, 2)),
            dma((STEPS, 2, 2)),
            dma((STEPS, 2, 2)),
            dma((2, 2, fields)),
            dma((2, 2, fields)),
        ],
        name="sphere_steps",
        compiler_params=pltpu.CompilerParams(collective_id=0, has_side_effects=True, vmem_limit_bytes=66_200_000),
    )(thickness, wind_field, *consts)


def solution(mesh):
    sizes = (mesh.shape["lon"], mesh.shape["lev"])
    in_specs = (P("lev", "lon", None), P(None, "lev", "lon", None))
    out_specs = (P("lev", "lon", None), P(None, "lev", "lon", None))
    return jax.shard_map(
        functools.partial(body, sizes), mesh=mesh, in_specs=in_specs, out_specs=out_specs, check_vma=False
    )
```
